32 devices in a mesh: expert: 16 (over z, y, x), replica: 2 (over core).
Axes of the slice: x: 2, y: 2, z: 4, core: 2. Of those that a mesh axis runs over, the one named last changes fastest.
Arguments:
- tokens: bfloat16 [1024, 7168], P('expert', 'replica'), may hold values from -6 to 6
- routes: int32 [1024, 8], P('expert'), may hold values from 0 to 15, all different within a row; in each aligned block of 64 rows (0 to 63, 64 to 127, ...) at most 64 rows name the same one
- route_scores: float32 [1024, 8], P('expert'), may hold values from 0.05 to 1
- placement: int32 [16], replicated, may hold values from 0 to 15, each once
- w_in: bfloat16 [16, 7168, 2, 1024], P('expert', 'replica'), may hold values from -0.0625 to 0.0625
- w_out: bfloat16 [16, 1024, 7168], P('expert', None, 'replica'), may hold values from -0.1875 to 0.1875
Outputs:
- mixed: bfloat16 [1024, 7168], P('expert', 'replica')
The draws below stay inside these ranges and needn't reach their ends.
Inputs may be any that keep to these rules, and one draw needn't show every extreme that they name: `routes`: each row names 8 different logical experts. Among the 64 rows of each aligned block (the tokens of one index of the expert axis) no expert is named by more than 64 rows, a bound that some block reaches. `placement`: A permutation of the physical slots.
All inputs are finite; a program needn't handle non-finite values.
Results may differ from the reference program's by a relative error of at most 0.0057.
Values may be sent and summed in bfloat16 or wider, within the bound.
A program may use at most 128 MiB of HBM per device.

```python
import math
import jax
import jax.numpy as jnp
import numpy as np
from jax import lax

D = 7168
FF = 1024
TOP = 8
TOK_DEV = 64
EXPERTS = 16
CAP = 64
TOKENS = 1024
N_EXPERT = 16


def block_levels(own_key, extent, split, smallest, largest):
    gain = 1.0
    for axis_at, blocks in split:
        heights = jax.random.uniform(jax.random.fold_in(jax.random.fold_in(own_key, 6), axis_at), (blocks,), jnp.float32, smallest / len(split), largest / len(split))
        gain = gain * jnp.repeat(jnp.exp(heights), extent[axis_at] // blocks).reshape((-1,) + (1,) * (len(extent) - 1 - axis_at))
    return gain


def shared_out(rng, own, number, rows, count, top, reach, skew):
    sequence = jax.random.permutation(rng, count)
    crowded, ordinary = load_shares(count, rows * top, reach, skew, True), load_shares(count, rows * top, reach, skew, False)
    places = jnp.arange(count)

    def named(lengths, turn):
        used = int((lengths > 0).sum())
        fixed = max(1, used // 4)
        passed = fixed + (places - fixed + turn * (used - fixed)) % max(1, count - fixed)
        return jnp.zeros((count,), jnp.int32).at[sequence[jnp.where(places < fixed, places, passed)]].set(jnp.asarray(lengths, jnp.int32))

    lengths = jnp.where(number % 4 == 0, named(crowded, number // 4), named(ordinary, number - number // 4 - 1))
    mixed = jax.random.permutation(jax.random.fold_in(own, 3), count)
    source_of, taker = mixed[0:count // 2 * 2:2], mixed[1:count // 2 * 2:2]
    room = jnp.minimum(lengths[source_of] - 1, reach - lengths[taker]) // 2
    room = jnp.where((source_of == sequence[0]) | (taker == sequence[0]) | (lengths[taker] == 0), 0, jnp.maximum(room, 0))
    passed = jax.random.randint(jax.random.fold_in(own, 4), (count // 2,), 0, 1 << 20) % (room + 1)
    lengths = lengths.at[source_of].add(-passed).at[taker].add(passed)
    items = jnp.searchsorted(jnp.cumsum(lengths), jnp.arange(rows * top), side="right").astype(jnp.int32)
    listing = items.reshape(top, rows).T
    listing = listing[jax.random.permutation(jax.random.fold_in(own, 1), rows)]
    turn = jax.random.randint(jax.random.fold_in(own, 2), (rows, 1), 0, top)
    return jnp.take_along_axis(listing, (jnp.arange(top)[None, :] + turn) % top, axis=1)


def load_shares(number_of, total, reach, slope, full):
    weights = [(1 << 20) // math.isqrt(standing ** slope) + 1 for standing in range(1, number_of + 1)]
    largest = reach if full else min(reach, max(-(-total // number_of), total * weights[0] // sum(weights)))
    least = 1 if total - largest >= number_of - 1 else 0
    counts, rest = [largest] + [least] * (number_of - 1), total - largest - least * (number_of - 1)
    while rest > 0:
        free = [i for i in range(1, number_of) if counts[i] < largest] or [i for i in range(1, number_of) if counts[i] < reach]
        pool, budget = sum([weights[i] for i in free]), rest
        for i in free:
            addition = min(reach - counts[i], max(1, budget * weights[i] // pool), rest)
            counts[i] = counts[i] + addition
            rest = rest - addition
    return np.array(counts)


def centred(own_key, dims, spread, reach, cuts=(), held_as=jnp.bfloat16):
    values = spread * jax.random.normal(own_key, dims, jnp.float32)
    if cuts:
        values = values * block_levels(own_key, dims, cuts, -0.22, 0.18)
    return jnp.clip(values, -reach, reach).astype(held_as)


def setup_inputs(seed: int = 0) -> dict:
    splits = jax.random.split(jax.random.key(seed), 7)
    tokens = centred(splits[0], (TOKENS, D), 1.0, 6.0, ((0, 16), (1, 2)))
    routes_keys = jax.random.split(jax.random.fold_in(splits[1], 1), TOKENS // TOK_DEV)
    routes_turns = jax.random.permutation(jax.random.fold_in(splits[1], 3), TOKENS // TOK_DEV)
    routes = jax.vmap(lambda own, number: shared_out(jax.random.fold_in(splits[1], 2), own, number, TOK_DEV, EXPERTS, TOP, CAP, 2))(routes_keys, routes_turns).reshape((TOKENS, TOP))
    route_scores = jnp.clip(jnp.exp(math.log(1.0) - 2.9957323 * jax.random.uniform(splits[2], (TOKENS, TOP), jnp.float32) ** block_levels(splits[2], (TOKENS, TOP), ((0, 16),), -0.2, 0.2)), 0.05, 1.0)
    placement = jax.random.permutation(splits[3], EXPERTS).astype(jnp.int32)
    w_in = centred(splits[4], (EXPERTS, D, 2, FF), D ** -0.5, 0.0625, ((0, 16), (1, 2)))
    w_out = centred(splits[5], (EXPERTS, FF, D), FF ** -0.5, 0.1875, ((0, 16), (2, 2)))
    return dict(tokens=tokens, routes=routes, route_scores=route_scores, placement=placement, w_in=w_in, w_out=w_out)


def reference(tokens, routes, route_scores, placement, w_in, w_out):
    physical = placement[routes]
    route_weight = 2.5 * route_scores / jnp.sum(route_scores, axis=1, keepdims=True)
    bound = N_EXPERT * CAP
    feature_cols = tokens.shape[1]

    def accumulate(running, expert):
        chosen = physical == expert
        member_weight = jnp.sum(jnp.where(chosen, route_weight, jnp.float32(0.0)), axis=1)
        taken = jnp.any(chosen, axis=1)
        members = jnp.nonzero(taken, size=bound, fill_value=0)[0]
        filled = jnp.arange(bound) < jnp.sum(taken.astype(jnp.int32))
        gathered = tokens[members]
        weights_in = lax.dynamic_index_in_dim(w_in, expert, 0, keepdims=False).reshape(feature_cols, 2 * FF)
        weights_out = lax.dynamic_index_in_dim(w_out, expert, 0, keepdims=False)
        pre_act = jnp.dot(gathered, weights_in, preferred_element_type=jnp.float32).reshape(bound, 2, FF)
        active = (jax.nn.silu(pre_act[:, 0]) * pre_act[:, 1]).astype(jnp.bfloat16)
        expert_out = jnp.dot(active, weights_out, preferred_element_type=jnp.float32).astype(jnp.bfloat16)
        expert_out = lax.optimization_barrier(expert_out).astype(jnp.float32)
        scale = jnp.where(filled, member_weight[members], jnp.float32(0.0))
        return running.at[members].add(expert_out * scale[:, None]), None

    mixed, unused = lax.scan(accumulate, jnp.zeros(tokens.shape, jnp.float32), jnp.arange(EXPERTS, dtype=jnp.int32))
    return mixed.astype(jnp.bfloat16)
```

```python
import jax
import jax.numpy as jnp
from jax import lax
from jax.experimental import pallas as pl
from jax.experimental.pallas import tpu as pltpu
from jax.sharding import PartitionSpec as P

LANES = 128
TILE = 256
MESH = pl.DeviceIdType.MESH
LINE = 4


def packed(tokens, routes, route_scores, placement, w_in, w_out):
    tok_rows, feature_cols = tokens.shape
    route_count = routes.shape[1]
    experts = placement.shape[0]
    hidden_units = w_in.shape[3]
    capacity = min(tok_rows, max(2, 2 * tok_rows * route_count // experts))
    slot_total = experts * capacity
    expert_ids = jnp.arange(experts, dtype=jnp.int32)
    route_table = routes[:, :, None] == expert_ids
    physical = jnp.sum(jnp.where(route_table, placement, 0), axis=-1)
    flat_slots = physical.reshape(-1)
    onehot = (flat_slots[:, None] == expert_ids).astype(jnp.int32)
    earlier = jnp.sum((jnp.cumsum(onehot, axis=0) - onehot) * onehot, axis=1)
    position = (flat_slots * capacity + earlier).reshape(tok_rows, route_count)
    slot_index = jnp.arange(slot_total, dtype=jnp.int32)
    placing = jnp.any(position[None, :, :] == slot_index[:, None, None], axis=-1).astype(
        jnp.bfloat16
    )
    outgoing = jnp.dot(placing, tokens, preferred_element_type=jnp.float32).astype(jnp.bfloat16)
    incoming = lax.all_to_all(outgoing, "expert", split_axis=0, concat_axis=0, tiled=True)
    weights_in = w_in[0].reshape(feature_cols, 2 * hidden_units)
    weights_out = w_out[0]
    partial_value = jnp.dot(incoming, weights_in, preferred_element_type=jnp.float32)
    partial_value = partial_value.reshape(slot_total, 2, hidden_units)
    shares = lax.psum_scatter(partial_value, "replica", scatter_dimension=2, tiled=True)
    active = (jax.nn.silu(shares[:, 0]) * shares[:, 1]).astype(jnp.bfloat16)
    result = jnp.dot(
        lax.all_gather(active, "replica", axis=1, tiled=True),
        weights_out,
        preferred_element_type=jnp.float32,
    )
    expert_out = result.astype(jnp.bfloat16)
    returned = lax.all_to_all(expert_out, "expert", split_axis=0, concat_axis=0, tiled=True)
    route_weight = 2.5 * route_scores / jnp.sum(route_scores, axis=1, keepdims=True)
    picked = returned[position.reshape(-1)].reshape(tok_rows, route_count, feature_cols)
    mixed = jnp.sum(picked.astype(jnp.float32) * route_weight[:, :, None], axis=1)
    return mixed.astype(jnp.bfloat16)


def expert_weights(routes, route_scores, placement):
    experts = placement.shape[0]
    expert_ids = jnp.arange(experts, dtype=jnp.int32)
    physical = jnp.sum(jnp.where(routes[:, :, None] == expert_ids, placement, 0), axis=-1)
    route_weight = 2.5 * route_scores / jnp.sum(route_scores, axis=1, keepdims=True)
    return jnp.sum(
        jnp.where(physical[:, :, None] == expert_ids, route_weight[:, :, None], 0.0), axis=1
    )


def layer_kernel(
    ext_ref, w_in_ref, w_out_ref, out_ref,
    xs, wg, wu, stage, wo, contrib, from_b, from_a, from_z, part, sent, got, act,
    w_sem, wo_sem, z_send, a_send, b_send, x_recv,
    p_send, p_recv, rb_send, rb_recv, ra_send, ra_recv, rz_send, rz_recv,
):
    rows, width = ext_ref.shape
    cols = out_ref.shape[1]
    hidden = wg.shape[1]
    tiles = hidden // TILE
    me = lax.axis_index("expert")
    core = lax.axis_index("replica")
    x, y, z = me % 2, (me // 2) % 2, me // 4
    flip_x, flip_y = me + 1 - 2 * x, me + 2 - 4 * y
    near_a = (1 - core) * flip_x + core * flip_y
    near_b = (1 - core) * flip_y + core * flip_x
    base = me - 4 * z

    def line(d):
        return (z + d) % LINE

    barrier = pltpu.get_barrier_semaphore()
    peers = [(near_a, core), (near_b, core), (me, 1 - core)]
    peers += [(base + 4 * line(d), core) for d in range(1, LINE)]
    for peer in peers:
        pl.semaphore_signal(barrier, inc=1, device_id=peer, device_id_type=MESH)
    pl.semaphore_wait(barrier, len(peers))

    def remote(src, dst, send, recv, chip, on_core=None):
        return pltpu.make_async_remote_copy(
            src_ref=src, dst_ref=dst, send_sem=send, recv_sem=recv,
            device_id=(chip, core if on_core is None else on_core), device_id_type=MESH,
        )

    def arrived(ref, recv):
        remote(ref, ref, a_send.at[0, 0], recv, near_a).wait_recv()

    def stage_copy(ct):
        return pltpu.make_async_copy(
            w_in_ref.at[0, :, :, pl.ds(ct * LANES, LANES)], stage.at[ct % 2], w_sem.at[ct % 2]
        )

    pending = []

    def go(copy):
        copy.start()
        pending.append(copy)

    part_rows = rows // 2

    def pass_on(source, to, send, chip, h):
        part = pl.ds(h * part_rows, part_rows)
        go(remote(source, xs.at[to, part], send.at[h], x_recv.at[to, h], chip))

    def landed(slot, h):
        part = pl.ds(h * part_rows, part_rows)
        arrived(xs.at[slot, part], x_recv.at[slot, h])
        return xs.at[slot, part]

    for h in range(2):
        own = ext_ref.at[pl.ds(h * part_rows, part_rows)]
        pass_on(own, LINE + z, a_send.at[0], near_a, h)
        pass_on(own, 2 * LINE + z, b_send.at[0], near_b, h)
        for d in (1, 3, 2):
            pass_on(own, z, z_send.at[d - 1], base + 4 * line(d), h)
    stage_copy(0).start()
    stage_copy(1).start()
    out_weights = pltpu.make_async_copy(w_out_ref.at[0], wo, wo_sem)
    out_weights.start()
    xs[z] = ext_ref[...]

    half = TILE // 2

    def sort_tile(ct):
        stage_copy(ct).wait()
        at_cols = slice(ct * LANES, (ct + 1) * LANES)

        def body(k, carry):
            at = pl.ds(pl.multiple_of(k * half, half), half)
            wg[at, at_cols] = stage[ct % 2, at, 0, :]
            wu[at, at_cols] = stage[ct % 2, at, 1, :]
            return carry

        lax.fori_loop(0, cols // half, body, 0)
        if ct + 2 < hidden // LANES:
            stage_copy(ct + 2).start()

    def own_line_on(d, n):
        slot = line(d)
        for h in range(2):
            held = landed(slot, h)
            pass_on(held, LINE + slot, a_send.at[n], near_a, h)
            pass_on(held, 2 * LINE + slot, b_send.at[n], near_b, h)

    def a_line_on(d, n):
        slot = LINE + line(d)
        for h in range(2):
            held = landed(slot, h)
            pass_on(held, 2 * LINE + slot, b_send.at[LINE + n], near_b, h)

    all_tiles = list(range(hidden // LANES))
    quarter = max(1, len(all_tiles) // 4)
    for ct in all_tiles[:2 * quarter]:
        sort_tile(ct)
    own_line_on(1, 1)
    a_line_on(0, 0)
    for ct in all_tiles[2 * quarter:3 * quarter]:
        sort_tile(ct)
    own_line_on(3, 2)
    a_line_on(1, 1)
    for ct in all_tiles[3 * quarter:]:
        sort_tile(ct)
    own_line_on(2, 3)
    a_line_on(3, 2)
    a_line_on(2, 3)
    out_weights.wait()

    lane = lax.broadcasted_iota(jnp.int32, (LINE * rows, LANES), 1)
    mine = (lane % 16 == me) & (lane < 48)

    def exchange(s, j):
        return remote(sent.at[s, j], got.at[s, j], p_send.at[s, j], p_recv.at[s, j], me, 1 - core)

    def step(s, group, ship=None):
        block = pl.ds(group * LINE, LINE)

        def first(j, carry):
            at = pl.ds(pl.multiple_of(j * TILE, TILE), TILE)
            value = xs[block, :, :cols].reshape(LINE * rows, cols)
            gate = jnp.dot(value, wg[:, at], preferred_element_type=jnp.float32)
            up = jnp.dot(value, wu[:, at], preferred_element_type=jnp.float32)
            part[j, 0] = gate
            part[j, 1] = up
            sent[s, j, 0] = gate.astype(jnp.bfloat16)
            sent[s, j, 1] = up.astype(jnp.bfloat16)
            exchange(s, j).start()
            return carry

        lax.fori_loop(0, tiles, first, 0)

        def second(j, carry):
            exchange(s, j).wait_recv()
            gate = part[j, 0] + got[s, j, 0].astype(jnp.float32)
            up = part[j, 1] + got[s, j, 1].astype(jnp.float32)
            act[:, pl.ds(pl.multiple_of(j * TILE, TILE), TILE)] = (
                gate / (1.0 + jnp.exp(-gate)) * up
            ).astype(jnp.bfloat16)
            return carry

        lax.fori_loop(0, tiles, second, 0)
        scales = xs[block, :, cols:].reshape(LINE * rows, LANES).astype(jnp.float32)
        scale = jnp.sum(jnp.where(mine, scales, 0.0), axis=1, keepdims=True)

        def third(j, carry):
            at = pl.ds(pl.multiple_of(j * TILE, TILE), TILE)
            value = jnp.dot(act[...], wo[:, at], preferred_element_type=jnp.float32)
            value = value * scale
            contrib[block, :, at] = value.astype(jnp.bfloat16).reshape(LINE, rows, TILE)
            return carry

        out_tiles = wide // TILE
        for h in range(2):
            lax.fori_loop(h * out_tiles, (h + 1) * out_tiles, third, 0)
            if ship is not None:
                ship(h)

    wide = cols // 2
    order = (1, 3, 2, 0)

    def cut(h):
        return slice(h * wide, (h + 1) * wide)

    def ship_b(from_line, to_line, h):
        for n, d in enumerate(order):
            src, to = from_line * LINE + line(d), to_line * LINE + line(d)
            go(remote(contrib.at[src, :, cut(h)], from_b.at[to, :, cut(h)],
                      rb_send.at[to_line * LINE + n, h], rb_recv.at[to, h], near_b))

    step(0, 0)
    for d in range(LINE):
        for h in range(2):
            landed(2 * LINE + line(d), h)
    step(1, 1 + core)
    step(2, 2 - core)
    for h in range(2):
        ship_b(2, 0, h)
    for d in range(LINE):
        for h in range(2):
            landed(3 * LINE + line(d), h)
    step(3, 3, lambda h: ship_b(3, 1, h))

    def plus(values):
        total = values[0].astype(jnp.float32)
        for value in values[1:]:
            total = total + value.astype(jnp.float32)
        return total

    def to_a(h, n, d):
        slot, to = LINE + line(d), line(d)
        arrived(from_b.at[slot, :, cut(h)], rb_recv.at[slot, h])
        contrib[slot, :, cut(h)] = plus(
            [contrib[slot, :, cut(h)], from_b[slot, :, cut(h)]]
        ).astype(jnp.bfloat16)
        go(remote(contrib.at[slot, :, cut(h)], from_a.at[to, :, cut(h)],
                  ra_send.at[n, h], ra_recv.at[to, h], near_a))

    def to_z(h, n, d):
        slot = line(d)
        arrived(from_b.at[slot, :, cut(h)], rb_recv.at[slot, h])
        arrived(from_a.at[slot, :, cut(h)], ra_recv.at[slot, h])
        contrib[slot, :, cut(h)] = plus(
            [contrib[slot, :, cut(h)], from_b[slot, :, cut(h)], from_a[slot, :, cut(h)]]
        ).astype(jnp.bfloat16)
        if d:
            to = LINE - 1 - d
            go(remote(contrib.at[slot, :, cut(h)], from_z.at[to, :, cut(h)],
                      rz_send.at[n, h], rz_recv.at[to, h], base + 4 * slot))

    for n, d in enumerate(order):
        to_a(0, n, d)
    for n, d in enumerate(order):
        to_a(1, n, d)
        to_z(0, n, d)
    for n, d in enumerate(order):
        to_z(1, n, d)
    for h in range(2):
        for d in range(LINE - 1):
            arrived(from_z.at[d, :, cut(h)], rz_recv.at[d, h])
        out_ref[:, cut(h)] = plus(
            [contrib[z, :, cut(h)]] + [from_z[d, :, cut(h)] for d in range(LINE - 1)]
        ).astype(jnp.bfloat16)
    for copy in pending:
        copy.wait_send()

    def drain(n, carry):
        exchange(n // tiles, n % tiles).wait_send()
        return carry

    lax.fori_loop(0, LINE * tiles, drain, 0)


def fused(tokens, routes, route_scores, placement, w_in, w_out):
    rows, cols = tokens.shape
    hidden = w_in.shape[3]
    tiles = hidden // TILE
    table = expert_weights(routes, route_scores, placement)
    high = lax.reduce_precision(table, 8, 7)
    middle = lax.reduce_precision(table - high, 8, 7)
    low = table - high - middle
    thirds = [third.astype(jnp.bfloat16) for third in (high, middle, low)]
    filler = jnp.zeros((rows, LANES - 3 * table.shape[1]), jnp.bfloat16)
    ext = jnp.concatenate([tokens, *thirds, filler], axis=1)
    slots = LINE * LINE
    bf16 = jnp.bfloat16
    dma = pltpu.SemaphoreType.DMA
    return pl.pallas_call(
        layer_kernel,
        out_shape=jax.ShapeDtypeStruct((rows, cols), bf16),
        in_specs=[
            pl.BlockSpec(memory_space=pltpu.VMEM),
            pl.BlockSpec(memory_space=pl.ANY),
            pl.BlockSpec(memory_space=pl.ANY),
        ],
        out_specs=pl.BlockSpec(memory_space=pltpu.VMEM),
        scratch_shapes=[
            pltpu.VMEM((slots, rows, cols + LANES), bf16),
            pltpu.VMEM((cols, hidden), bf16),
            pltpu.VMEM((cols, hidden), bf16),
            pltpu.VMEM((2, cols, 2, LANES), bf16),
            pltpu.VMEM((hidden, cols), bf16),
            pltpu.VMEM((slots, rows, cols), bf16),
            pltpu.VMEM((2 * LINE, rows, cols), bf16),
            pltpu.VMEM((LINE, rows, cols), bf16),
            pltpu.VMEM((LINE - 1, rows, cols), bf16),
            pltpu.VMEM((tiles, 2, LINE * rows, TILE), jnp.float32),
            pltpu.VMEM((LINE, tiles, 2, LINE * rows, TILE), bf16),
            pltpu.VMEM((LINE, tiles, 2, LINE * rows, TILE), bf16),
            pltpu.VMEM((LINE * rows, hidden), bf16),
            dma((2,)), dma, dma((LINE - 1, 2)), dma((LINE, 2)), dma((2 * LINE, 2)), dma((slots, 2)),
            dma((LINE, tiles)), dma((LINE, tiles)),
            dma((2 * LINE, 2)), dma((2 * LINE, 2)), dma((LINE, 2)), dma((LINE, 2)),
            dma((LINE, 2)), dma((LINE - 1, 2)),
        ],
        compiler_params=pltpu.CompilerParams(
            collective_id=0, has_side_effects=True, vmem_limit_bytes=67043328
        ),
    )(ext, w_in, w_out)


def on_device(tokens, routes, route_scores, placement, w_in, w_out):
    tok_rows = tokens.shape[0]
    experts = placement.shape[0]
    fits = experts == 4 * LINE and lax.axis_size("replica") == 2
    if fits and 2 * tok_rows * routes.shape[1] // experts >= tok_rows:
        return fused(tokens, routes, route_scores, placement, w_in, w_out)
    return packed(tokens, routes, route_scores, placement, w_in, w_out)


def solution(mesh):
    in_specs = (
        P("expert", "replica"),
        P("expert", None),
        P("expert", None),
        P(),
        P("expert", "replica", None, None),
        P("expert", None, "replica"),
    )
    out_specs = P("expert", "replica")
    return jax.shard_map(
        on_device, mesh=mesh, in_specs=in_specs, out_specs=out_specs, check_vma=False
    )
```

```python
import functools

import jax
import jax.numpy as jnp
from jax import lax
from jax.experimental import pallas as pl
from jax.experimental.pallas import tpu as pltpu
from jax.sharding import PartitionSpec as P

LANES = 128
TILE = 256
WIDE_TILE = 512
MESH = pl.DeviceIdType.MESH
LINE = 4
OWN, SIDE_A, SIDE_B, DIAGONAL = range(4)
UP, DOWN = range(2)
TO_A, TO_B, TO_UP, TO_DOWN = range(4)
NEAREST = ((0, 1, 2, 3), (1, 0, 2, 3), (2, 3, 1, 0), (3, 2, 1, 0))
ENDS, INNER, EVERY = (0, LINE - 1), (1, 2), (0, 1, 2, 3)


def slot_of(line, rank):
    if line == OWN:
        return rank
    if line == DIAGONAL:
        return 3 * LINE + rank
    return LINE * (1 + rank // 2) + 2 * (line - 1) + rank % 2


def packed(tokens, routes, route_scores, placement, w_in, w_out):
    tok_rows, feature_cols = tokens.shape
    route_count = routes.shape[1]
    experts = placement.shape[0]
    hidden_units = w_in.shape[3]
    capacity = min(tok_rows, max(2, 2 * tok_rows * route_count // experts))
    slot_total = experts * capacity
    expert_ids = jnp.arange(experts, dtype=jnp.int32)
    route_table = routes[:, :, None] == expert_ids
    physical = jnp.sum(jnp.where(route_table, placement, 0), axis=-1)
    flat_slots = physical.reshape(-1)
    onehot = (flat_slots[:, None] == expert_ids).astype(jnp.int32)
    earlier = jnp.sum((jnp.cumsum(onehot, axis=0) - onehot) * onehot, axis=1)
    position = (flat_slots * capacity + earlier).reshape(tok_rows, route_count)
    slot_index = jnp.arange(slot_total, dtype=jnp.int32)
    placing = jnp.any(position[None, :, :] == slot_index[:, None, None], axis=-1).astype(
        jnp.bfloat16
    )
    outgoing = jnp.dot(placing, tokens, preferred_element_type=jnp.float32).astype(jnp.bfloat16)
    incoming = lax.all_to_all(outgoing, "expert", split_axis=0, concat_axis=0, tiled=True)
    weights_in = w_in[0].reshape(feature_cols, 2 * hidden_units)
    weights_out = w_out[0]
    partial_value = jnp.dot(incoming, weights_in, preferred_element_type=jnp.float32)
    partial_value = partial_value.reshape(slot_total, 2, hidden_units)
    shares = lax.psum_scatter(partial_value, "replica", scatter_dimension=2, tiled=True)
    active = (jax.nn.silu(shares[:, 0]) * shares[:, 1]).astype(jnp.bfloat16)
    result = jnp.dot(
        lax.all_gather(active, "replica", axis=1, tiled=True),
        weights_out,
        preferred_element_type=jnp.float32,
    )
    expert_out = result.astype(jnp.bfloat16)
    returned = lax.all_to_all(expert_out, "expert", split_axis=0, concat_axis=0, tiled=True)
    route_weight = 2.5 * route_scores / jnp.sum(route_scores, axis=1, keepdims=True)
    picked = returned[position.reshape(-1)].reshape(tok_rows, route_count, feature_cols)
    mixed = jnp.sum(picked.astype(jnp.float32) * route_weight[:, :, None], axis=1)
    return mixed.astype(jnp.bfloat16)


def expert_weights(routes, route_scores, placement):
    experts = placement.shape[0]
    expert_ids = jnp.arange(experts, dtype=jnp.int32)
    physical = jnp.sum(jnp.where(routes[:, :, None] == expert_ids, placement, 0), axis=-1)
    route_weight = 2.5 * route_scores / jnp.sum(route_scores, axis=1, keepdims=True)
    return jnp.sum(
        jnp.where(physical[:, :, None] == expert_ids, route_weight[:, :, None], 0.0), axis=1
    )


def layer_kernel(
    ext_ref, w_in_ref, w_out_ref, out_ref,
    xs, wg, wu, stage, wo, contrib, z_in, a_in, b_in, part, sent, got, act,
    w_sem, wo_sem, x_send, x_recv, p_send, p_recv,
    z_send, z_recv, a_send, a_recv, b_send, b_recv,
):
    rows, width = ext_ref.shape
    cols = out_ref.shape[1]
    hidden = wg.shape[1]
    tiles = hidden // TILE
    me = lax.axis_index("expert")
    core = lax.axis_index("replica")
    x, y, z = me % 2, (me // 2) % 2, me // 4
    flip_x, flip_y = me + 1 - 2 * x, me + 2 - 4 * y
    near_a = (1 - core) * flip_x + core * flip_y
    near_b = (1 - core) * flip_y + core * flip_x
    chips = (near_a, near_b, me + 4, me - 4)
    sends = {plane: [] for plane in EVERY}

    def on(planes, act_on):
        for plane in planes:
            pl.when(z == plane)(functools.partial(act_on, plane))

    def remote(src, dst, send, recv, chip, on_core=None):
        return pltpu.make_async_remote_copy(
            src_ref=src, dst_ref=dst, send_sem=send, recv_sem=recv,
            device_id=(chip, core if on_core is None else on_core), device_id_type=MESH,
        )

    def arrived(ref, recv):
        remote(ref, ref, a_send.at[0, 0], recv, near_a).wait_recv()

    barrier = pltpu.get_barrier_semaphore()
    for peer in ((near_a, core), (near_b, core), (me, 1 - core)):
        pl.semaphore_signal(barrier, inc=1, device_id=peer, device_id_type=MESH)

    def greet(plane):
        for step, there in ((4, plane + 1), (-4, plane - 1)):
            if 0 <= there < LINE:
                pl.semaphore_signal(
                    barrier, inc=1, device_id=(me + step, core), device_id_type=MESH
                )
        pl.semaphore_wait(barrier, 4 if plane in ENDS else 5)

    on(EVERY, greet)

    def start(plane, copy):
        copy().start()
        sends[plane].append(copy)

    part_rows = rows // 2

    def piece(h):
        return pl.ds(h * part_rows, part_rows)

    def ship(plane, source, from_slot, to_slot, kind, h):
        start(plane, lambda: remote(
            source(), xs.at[to_slot, piece(h)], x_send.at[kind, from_slot, h],
            x_recv.at[to_slot, h], chips[kind]))

    def landed(slot, h):
        arrived(xs.at[slot, piece(h)], x_recv.at[slot, h])
        return lambda: xs.at[slot, piece(h)]

    def ship_along(plane, source, line, rank, h):
        there = NEAREST[plane][rank]
        slot = slot_of(line, rank)
        if plane < LINE - 1 and there <= plane:
            ship(plane, source, slot, slot_of(line, NEAREST[plane + 1].index(there)), TO_UP, h)
        if plane > 0 and there >= plane:
            ship(plane, source, slot, slot_of(line, NEAREST[plane - 1].index(there)), TO_DOWN, h)

    def own_piece(h):
        return ext_ref.at[piece(h)]

    def send_own(plane):
        for h in range(2):
            source = functools.partial(own_piece, h)
            ship(plane, source, 0, slot_of(SIDE_A, 0), TO_A, h)
            ship(plane, source, 0, slot_of(SIDE_B, 0), TO_B, h)
            ship_along(plane, source, OWN, 0, h)

    def relay_own(rank):
        def act_on(plane):
            slot = slot_of(OWN, rank)
            for h in range(2):
                source = landed(slot, h)
                ship_along(plane, source, OWN, rank, h)
                ship(plane, source, slot, slot_of(SIDE_A, rank), TO_A, h)
                ship(plane, source, slot, slot_of(SIDE_B, rank), TO_B, h)
        return act_on

    def relay_side(plane):
        slot = slot_of(SIDE_A, 0)
        for h in range(2):
            ship(plane, landed(slot, h), slot, slot_of(DIAGONAL, 0), TO_B, h)

    def relay_diagonal(rank):
        def act_on(plane):
            for h in range(2):
                ship_along(plane, landed(slot_of(DIAGONAL, rank), h), DIAGONAL, rank, h)
        return act_on

    def wait_for(line, rank):
        for h in range(2):
            landed(slot_of(line, rank), h)

    def stage_copy(ct):
        return pltpu.make_async_copy(
            w_in_ref.at[0, :, :, pl.ds(ct * LANES, LANES)], stage.at[ct % 2], w_sem.at[ct % 2]
        )

    def sort_tile(ct):
        stage_copy(ct).wait()
        at_cols = slice(ct * LANES, (ct + 1) * LANES)

        def body(k, carry):
            at = pl.ds(pl.multiple_of(k * LANES, LANES), LANES)
            wg[at, at_cols] = stage[ct % 2, at, 0, :]
            wu[at, at_cols] = stage[ct % 2, at, 1, :]
            return carry

        lax.fori_loop(0, cols // LANES, body, 0)
        if ct + 2 < hidden // LANES:
            stage_copy(ct + 2).start()

    def exchange(s, first_slot, count, j):
        at = pl.ds(first_slot * rows, count * rows)
        return remote(sent.at[j, :, at], got.at[j, :, at], p_send.at[s, j], p_recv.at[s, j],
                      me, 1 - core)

    def project_in(s, first_slot, count):
        size = count * rows
        block = pl.ds(first_slot, count)
        at_rows = pl.ds(first_slot * rows, size)

        def body(j, carry):
            at = pl.ds(pl.multiple_of(j * TILE, TILE), TILE)
            value = xs[block, :, :cols].reshape(size, cols)
            gate = jnp.dot(value, wg[:, at], preferred_element_type=jnp.float32)
            up = jnp.dot(value, wu[:, at], preferred_element_type=jnp.float32)
            part[j, 0, :size] = gate
            part[j, 1, :size] = up
            for k, value in ((0, gate), (1, up)):
                value = value.astype(jnp.bfloat16)
                if LINE <= first_slot < 3 * LINE:
                    sent[j, k, pl.ds(first_slot * rows, size // 2)] = value[size // 2:]
                    sent[j, k, pl.ds(first_slot * rows + size // 2, size // 2)] = value[:size // 2]
                else:
                    sent[j, k, at_rows] = value
            exchange(s, first_slot, count, j).start()
            return carry

        lax.fori_loop(0, tiles, body, 0)

    def activate(s, first_slot, count):
        size = count * rows
        at_rows = pl.ds(first_slot * rows, size)

        def body(j, carry):
            exchange(s, first_slot, count, j).wait_recv()
            gate = part[j, 0, :size] + got[j, 0, at_rows].astype(jnp.float32)
            up = part[j, 1, :size] + got[j, 1, at_rows].astype(jnp.float32)
            act[:size, pl.ds(pl.multiple_of(j * TILE, TILE), TILE)] = (
                gate / (1.0 + jnp.exp(-gate)) * up
            ).astype(jnp.bfloat16)
            return carry

        lax.fori_loop(0, tiles, body, 0)

    wide_tiles = cols // WIDE_TILE
    bounds = (0, (wide_tiles + 1) // 2, wide_tiles)

    def cut(h):
        return pl.ds(bounds[h] * WIDE_TILE, (bounds[h + 1] - bounds[h]) * WIDE_TILE)

    def project_out(first_slot, count, h):
        size = count * rows
        block = pl.ds(first_slot, count)
        lane = lax.broadcasted_iota(jnp.int32, (size, LANES), 1)
        mine = (lane % 16 == me) & (lane < 48)
        scales = xs[block, :, cols:].reshape(size, LANES).astype(jnp.float32)
        scale = jnp.sum(jnp.where(mine, scales, 0.0), axis=1, keepdims=True)

        def body(j, carry):
            at = pl.ds(pl.multiple_of(j * WIDE_TILE, WIDE_TILE), WIDE_TILE)
            value = jnp.dot(act[:size], wo[:, at], preferred_element_type=jnp.float32)
            value = value * scale
            contrib[block, :, at] = value.astype(jnp.bfloat16).reshape(count, rows, WIDE_TILE)
            return carry

        lax.fori_loop(bounds[h], bounds[h + 1], body, 0)

    def add_up(h, target, terms):
        def body(j, carry):
            at = pl.ds(pl.multiple_of(j * WIDE_TILE, WIDE_TILE), WIDE_TILE)
            total = terms[0][:, at].astype(jnp.float32)
            for term in terms[1:]:
                total = total + term[:, at].astype(jnp.float32)
            target[:, at] = total.astype(jnp.bfloat16)
            return carry

        lax.fori_loop(bounds[h], bounds[h + 1], body, 0)

    def pass_sum(plane, h, slot, target, send, recv, chip):
        start(plane, lambda: remote(
            contrib.at[slot, :, cut(h)], target[0].at[target[1]].at[:, cut(h)],
            send.at[(*target[1], h)], recv.at[(*target[1], h)], chip))

    def cross(rank, h):
        pass_sum("all", h, slot_of(SIDE_B, rank), (a_in, (rank,)), a_send, a_recv, near_a)
        pass_sum("all", h, slot_of(SIDE_A, rank), (b_in, (rank,)), b_send, b_recv, near_b)

    def straight(h):
        pass_sum("all", h, slot_of(SIDE_B, 0), (b_in, (0,)), b_send, b_recv, near_b)

    sends["all"] = []

    def take(buffer, recv, index, h):
        arrived(buffer.at[(*index, slice(None), cut(h))], recv.at[(*index, h)])
        return buffer.at[index]

    def along(line, rank, h):
        kind = line // DIAGONAL

        def act_on(plane):
            there = NEAREST[plane][rank]
            way = UP if there > plane else DOWN
            far = abs(there - plane)
            slot = slot_of(line, rank)
            terms = [contrib.at[slot]]
            if line == DIAGONAL:
                terms.append(take(a_in, a_recv, (rank,), h))
                terms.append(take(b_in, b_recv, (rank,), h))
            if plane != (0 if way == UP else LINE - 1):
                terms.append(take(z_in, z_recv, (kind, way, far), h))
            if len(terms) > 1:
                add_up(h, contrib.at[slot], terms)
            pass_sum(plane, h, slot, (z_in, (kind, way, far - 1)), z_send, z_recv,
                     chips[TO_UP if way == UP else TO_DOWN])
        return act_on

    def from_line(plane, kind, h):
        return [
            take(z_in, z_recv, (kind, way, 0), h)
            for way, stop in ((UP, 0), (DOWN, LINE - 1)) if plane != stop
        ]

    def turn_b(h):
        def act_on(plane):
            slot = slot_of(DIAGONAL, 0)
            add_up(h, contrib.at[slot], [contrib.at[slot], *from_line(plane, 1, h)])
            pass_sum(plane, h, slot, (b_in, (LINE,)), b_send, b_recv, near_b)
        return act_on

    def turn_a(h):
        slot = slot_of(SIDE_A, 0)
        add_up(h, contrib.at[slot], [contrib.at[slot], take(b_in, b_recv, (LINE,), h)])
        pass_sum("all", h, slot, (a_in, (0,)), a_send, a_recv, near_a)

    def finish(h):
        def act_on(plane):
            terms = [contrib.at[0], take(b_in, b_recv, (0,), h), *from_line(plane, 0, h)]
            add_up(h, out_ref, [*terms, take(a_in, a_recv, (0,), h)])
        return act_on

    groups = ((0, 2), (2, 2), (4, 4), (8, 4), (12, 2), (14, 2))

    def begin(s):
        project_in(s, *groups[s])
        activate(s, *groups[s])

    def close(s, h):
        project_out(*groups[s], h)

    on(EVERY, send_own)
    stage_copy(0).start()
    stage_copy(1).start()
    out_weights = pltpu.make_async_copy(w_out_ref.at[0], wo, wo_sem)
    out_weights.start()
    xs[0] = ext_ref[...]
    for ct in range(hidden // LANES):
        sort_tile(ct)
    on(EVERY, relay_side)
    on(EVERY, relay_own(1))
    on(INNER, relay_own(2))
    begin(0)
    out_weights.wait()
    close(0, 0)
    close(0, 1)
    on(INNER, relay_own(3))
    on(ENDS, relay_own(2))
    on(EVERY, relay_diagonal(0))
    for h in range(2):
        on(ENDS, along(OWN, 1, h))
    on(ENDS, relay_own(3))
    begin(1)
    for h in range(2):
        close(1, h)
        on(ENDS, along(OWN, 3, h))
        on(ENDS, along(OWN, 2, h))
    on(INNER, relay_diagonal(1))
    on(INNER, relay_diagonal(2))
    for rank in range(2):
        if rank:
            wait_for(SIDE_A, rank)
        wait_for(SIDE_B, rank)
    begin(2)
    on(INNER, relay_diagonal(3))
    for h in range(2):
        close(2, h)
        cross(1, h)
    for h in range(2):
        on(INNER, along(OWN, 3, h))
    for rank in (2, 3):
        wait_for(SIDE_A, rank)
        wait_for(SIDE_B, rank)
    begin(3)
    for h in range(2):
        close(3, h)
        cross(3, h)
        cross(2, h)
    for h in range(2):
        on(INNER, along(OWN, 2, h))
    on(ENDS, lambda plane: wait_for(DIAGONAL, 1))
    begin(4)
    for h in range(2):
        close(4, h)
        straight(h)
        on(ENDS, along(DIAGONAL, 1, h))
    for h in range(2):
        on(INNER, along(OWN, 1, h))
    on(ENDS, lambda plane: wait_for(DIAGONAL, 2))
    on(ENDS, lambda plane: wait_for(DIAGONAL, 3))
    begin(5)
    for h in range(2):
        close(5, h)
        on(ENDS, along(DIAGONAL, 3, h))
        on(ENDS, along(DIAGONAL, 2, h))
    for h in range(2):
        on(INNER, along(DIAGONAL, 3, h))
    for h in range(2):
        on(INNER, along(DIAGONAL, 2, h))
    for h in range(2):
        on(INNER, along(DIAGONAL, 1, h))
    for h in range(2):
        on(EVERY, turn_b(h))
    for h in range(2):
        turn_a(h)
    for h in range(2):
        on(EVERY, finish(h))
    for copy in sends["all"]:
        copy().wait_send()

    def drained(plane):
        for copy in sends[plane]:
            copy().wait_send()

    on(EVERY, drained)
    for s, (first_slot, count) in enumerate(groups):
        def drain(j, carry):
            exchange(s, first_slot, count, j).wait_send()
            return carry

        lax.fori_loop(0, tiles, drain, 0)


def fused(tokens, routes, route_scores, placement, w_in, w_out):
    rows, cols = tokens.shape
    hidden = w_in.shape[3]
    tiles = hidden // TILE
    table = expert_weights(routes, route_scores, placement)
    high = lax.reduce_precision(table, 8, 7)
    middle = lax.reduce_precision(table - high, 8, 7)
    low = table - high - middle
    thirds = [third.astype(jnp.bfloat16) for third in (high, middle, low)]
    filler = jnp.zeros((rows, LANES - 3 * table.shape[1]), jnp.bfloat16)
    ext = jnp.concatenate([tokens, *thirds, filler], axis=1)
    slots = LINE * LINE
    bf16 = jnp.bfloat16
    dma = pltpu.SemaphoreType.DMA
    return pl.pallas_call(
        layer_kernel,
        out_shape=jax.ShapeDtypeStruct((rows, cols), bf16),
        in_specs=[
            pl.BlockSpec(memory_space=pltpu.VMEM),
            pl.BlockSpec(memory_space=pl.ANY),
            pl.BlockSpec(memory_space=pl.ANY),
        ],
        out_specs=pl.BlockSpec(memory_space=pltpu.VMEM),
        scratch_shapes=[
            pltpu.VMEM((slots, rows, cols + LANES), bf16),
            pltpu.VMEM((cols, hidden), bf16),
            pltpu.VMEM((cols, hidden), bf16),
            pltpu.VMEM((2, cols, 2, LANES), bf16),
            pltpu.VMEM((hidden, cols), bf16),
            pltpu.VMEM((slots, rows, cols), bf16),
            pltpu.VMEM((2, 2, LINE - 1, rows, cols), bf16),
            pltpu.VMEM((LINE, rows, cols), bf16),
            pltpu.VMEM((LINE + 1, rows, cols), bf16),
            pltpu.VMEM((tiles, 2, LINE * rows, TILE), jnp.float32),
            pltpu.VMEM((tiles, 2, slots * rows, TILE), bf16),
            pltpu.VMEM((tiles, 2, slots * rows, TILE), bf16),
            pltpu.VMEM((LINE * rows, hidden), bf16),
            dma((2,)), dma, dma((4, slots, 2)), dma((slots, 2)),
            dma((slots, tiles)), dma((slots, tiles)),
            dma((2, 2, LINE - 1, 2)), dma((2, 2, LINE - 1, 2)),
            dma((LINE, 2)), dma((LINE, 2)), dma((LINE + 1, 2)), dma((LINE + 1, 2)),
        ],
        compiler_params=pltpu.CompilerParams(
            collective_id=0, has_side_effects=True, vmem_limit_bytes=67043328
        ),
    )(ext, w_in, w_out)


def on_device(tokens, routes, route_scores, placement, w_in, w_out):
    tok_rows = tokens.shape[0]
    experts = placement.shape[0]
    fits = experts == 4 * LINE and lax.axis_size("replica") == 2
    if fits and 2 * tok_rows * routes.shape[1] // experts >= tok_rows:
        return fused(tokens, routes, route_scores, placement, w_in, w_out)
    return packed(tokens, routes, route_scores, placement, w_in, w_out)


def solution(mesh):
    in_specs = (
        P("expert", "replica"),
        P("expert", None),
        P("expert", None),
        P(),
        P("expert", "replica", None, None),
        P("expert", None, "replica"),
    )
    out_specs = P("expert", "replica")
    return jax.shard_map(
        on_device, mesh=mesh, in_specs=in_specs, out_specs=out_specs, check_vma=False
    )
```

```python
import functools

import jax
import jax.numpy as jnp
from jax import lax
from jax.experimental import pallas as pl
from jax.experimental.pallas import tpu as pltpu
from jax.sharding import PartitionSpec as P

LANES = 128
TILE = 256
WIDE_TILE = 512
PIECES = 4
MESH = pl.DeviceIdType.MESH
LINE = 4
OWN, SIDE_A, SIDE_B, DIAGONAL = range(4)
UP, DOWN = range(2)
TO_A, TO_B, TO_UP, TO_DOWN = range(4)
NEAREST = ((0, 1, 2, 3), (1, 0, 2, 3), (2, 3, 1, 0), (3, 2, 1, 0))
ENDS, INNER, EVERY = (0, LINE - 1), (1, 2), (0, 1, 2, 3)
SLOTS = (
    (OWN, 0), (OWN, 1), (SIDE_A, 0), (SIDE_B, 0), (OWN, 2), (OWN, 3), (SIDE_A, 1), (SIDE_B, 1),
    (SIDE_A, 2), (SIDE_B, 2), (SIDE_A, 3), (SIDE_B, 3),
    (DIAGONAL, 0), (DIAGONAL, 1), (DIAGONAL, 2), (DIAGONAL, 3),
)


def slot_of(line, rank):
    return SLOTS.index((line, rank))


def twin_of(slot):
    line, rank = SLOTS[slot]
    return slot_of({SIDE_A: SIDE_B, SIDE_B: SIDE_A}.get(line, line), rank)


def packed(tokens, routes, route_scores, placement, w_in, w_out):
    tok_rows, feature_cols = tokens.shape
    route_count = routes.shape[1]
    experts = placement.shape[0]
    hidden_units = w_in.shape[3]
    capacity = min(tok_rows, max(2, 2 * tok_rows * route_count // experts))
    slot_total = experts * capacity
    expert_ids = jnp.arange(experts, dtype=jnp.int32)
    route_table = routes[:, :, None] == expert_ids
    physical = jnp.sum(jnp.where(route_table, placement, 0), axis=-1)
    flat_slots = physical.reshape(-1)
    onehot = (flat_slots[:, None] == expert_ids).astype(jnp.int32)
    earlier = jnp.sum((jnp.cumsum(onehot, axis=0) - onehot) * onehot, axis=1)
    position = (flat_slots * capacity + earlier).reshape(tok_rows, route_count)
    slot_index = jnp.arange(slot_total, dtype=jnp.int32)
    placing = jnp.any(position[None, :, :] == slot_index[:, None, None], axis=-1).astype(
        jnp.bfloat16
    )
    outgoing = jnp.dot(placing, tokens, preferred_element_type=jnp.float32).astype(jnp.bfloat16)
    incoming = lax.all_to_all(outgoing, "expert", split_axis=0, concat_axis=0, tiled=True)
    weights_in = w_in[0].reshape(feature_cols, 2 * hidden_units)
    weights_out = w_out[0]
    partial_value = jnp.dot(incoming, weights_in, preferred_element_type=jnp.float32)
    partial_value = partial_value.reshape(slot_total, 2, hidden_units)
    shares = lax.psum_scatter(partial_value, "replica", scatter_dimension=2, tiled=True)
    active = (jax.nn.silu(shares[:, 0]) * shares[:, 1]).astype(jnp.bfloat16)
    result = jnp.dot(
        lax.all_gather(active, "replica", axis=1, tiled=True),
        weights_out,
        preferred_element_type=jnp.float32,
    )
    expert_out = result.astype(jnp.bfloat16)
    returned = lax.all_to_all(expert_out, "expert", split_axis=0, concat_axis=0, tiled=True)
    route_weight = 2.5 * route_scores / jnp.sum(route_scores, axis=1, keepdims=True)
    picked = returned[position.reshape(-1)].reshape(tok_rows, route_count, feature_cols)
    mixed = jnp.sum(picked.astype(jnp.float32) * route_weight[:, :, None], axis=1)
    return mixed.astype(jnp.bfloat16)


def expert_weights(routes, route_scores, placement):
    experts = placement.shape[0]
    expert_ids = jnp.arange(experts, dtype=jnp.int32)
    physical = jnp.sum(jnp.where(routes[:, :, None] == expert_ids, placement, 0), axis=-1)
    route_weight = 2.5 * route_scores / jnp.sum(route_scores, axis=1, keepdims=True)
    return jnp.sum(
        jnp.where(physical[:, :, None] == expert_ids, route_weight[:, :, None], 0.0), axis=1
    )


def layer_kernel(
    ext_ref, w_in_ref, w_out_ref, out_ref,
    xs, wg, wu, stage, pairs, wo, contrib, z_in, a_in, b_in, part, sent, got, act,
    w_sem, wo_sem, x_send, x_recv, p_send, p_recv,
    z_send, z_recv, a_send, a_recv, b_send, b_recv,
):
    rows, width = ext_ref.shape
    cols = out_ref.shape[1]
    hidden = wg.shape[1]
    tiles = hidden // TILE
    me = lax.axis_index("expert")
    core = lax.axis_index("replica")
    x, y, z = me % 2, (me // 2) % 2, me // 4
    flip_x, flip_y = me + 1 - 2 * x, me + 2 - 4 * y
    near_a = (1 - core) * flip_x + core * flip_y
    near_b = (1 - core) * flip_y + core * flip_x
    chips = (near_a, near_b, me + 4, me - 4)
    sends = {plane: [] for plane in EVERY}

    def on(planes, act_on):
        for plane in planes:
            pl.when(z == plane)(functools.partial(act_on, plane))

    def remote(src, dst, send, recv, chip, on_core=None):
        return pltpu.make_async_remote_copy(
            src_ref=src, dst_ref=dst, send_sem=send, recv_sem=recv,
            device_id=(chip, core if on_core is None else on_core), device_id_type=MESH,
        )

    def arrived(ref, recv):
        remote(ref, ref, a_send.at[0, 0], recv, near_a).wait_recv()

    barrier = pltpu.get_barrier_semaphore()
    for peer in ((near_a, core), (near_b, core), (me, 1 - core)):
        pl.semaphore_signal(barrier, inc=1, device_id=peer, device_id_type=MESH)

    def greet(plane):
        for step, there in ((4, plane + 1), (-4, plane - 1)):
            if 0 <= there < LINE:
                pl.semaphore_signal(
                    barrier, inc=1, device_id=(me + step, core), device_id_type=MESH
                )
        pl.semaphore_wait(barrier, 4 if plane in ENDS else 5)

    on(EVERY, greet)

    def start(plane, copy):
        copy().start()
        sends[plane].append(copy)

    part_rows = rows // 2

    def piece(h):
        return pl.ds(h * part_rows, part_rows)

    def ship(plane, source, from_slot, to_slot, kind, h):
        start(plane, lambda: remote(
            source(), xs.at[to_slot, piece(h)], x_send.at[kind, from_slot, h],
            x_recv.at[to_slot, h], chips[kind]))

    def landed(slot, h):
        arrived(xs.at[slot, piece(h)], x_recv.at[slot, h])
        return lambda: xs.at[slot, piece(h)]

    def ship_along(plane, source, line, rank, h):
        there = NEAREST[plane][rank]
        slot = slot_of(line, rank)
        if plane < LINE - 1 and there <= plane:
            ship(plane, source, slot, slot_of(line, NEAREST[plane + 1].index(there)), TO_UP, h)
        if plane > 0 and there >= plane:
            ship(plane, source, slot, slot_of(line, NEAREST[plane - 1].index(there)), TO_DOWN, h)

    def own_piece(h):
        return ext_ref.at[piece(h)]

    def send_own(plane):
        for h in range(2):
            source = functools.partial(own_piece, h)
            ship(plane, source, 0, slot_of(SIDE_A, 0), TO_A, h)
            ship(plane, source, 0, slot_of(SIDE_B, 0), TO_B, h)
            ship_along(plane, source, OWN, 0, h)

    def relay_own(rank, h):
        def act_on(plane):
            slot = slot_of(OWN, rank)
            source = landed(slot, h)
            ship_along(plane, source, OWN, rank, h)
            ship(plane, source, slot, slot_of(SIDE_A, rank), TO_A, h)
            ship(plane, source, slot, slot_of(SIDE_B, rank), TO_B, h)
        return act_on

    def pass_z(rank, h):
        def act_on(plane):
            ship_along(plane, landed(slot_of(OWN, rank), h), OWN, rank, h)
        return act_on

    def pass_ab(rank, h):
        def act_on(plane):
            slot = slot_of(OWN, rank)

            def held():
                return xs.at[slot, piece(h)]

            ship(plane, held, slot, slot_of(SIDE_A, rank), TO_A, h)
            ship(plane, held, slot, slot_of(SIDE_B, rank), TO_B, h)
        return act_on

    def relay_side(h):
        def act_on(plane):
            slot = slot_of(SIDE_A, 0)
            ship(plane, landed(slot, h), slot, slot_of(DIAGONAL, 0), TO_B, h)
        return act_on

    def relay_diagonal(rank, h):
        def act_on(plane):
            ship_along(plane, landed(slot_of(DIAGONAL, rank), h), DIAGONAL, rank, h)
        return act_on

    def wait_for(line, rank):
        for h in range(2):
            landed(slot_of(line, rank), h)

    def stage_copy(ct):
        return pltpu.make_async_copy(
            w_in_ref.at[0, :, :, pl.ds(ct * LANES, LANES)], stage.at[ct % 2], w_sem.at[ct % 2]
        )

    def sort_tile(ct):
        stage_copy(ct).wait()
        at_cols = slice(ct * LANES, (ct + 1) * LANES)

        flat = stage.at[ct % 2].reshape(2 * cols, LANES)

        def body(k, carry):
            for n in range(2):
                first = pl.multiple_of((2 * k + n) * LANES, LANES)
                at = pl.ds(first, LANES)
                pairs[n] = flat[pl.ds(2 * first, 2 * LANES), :].astype(jnp.float32)
                wg[at, at_cols] = pairs[n, pl.ds(0, LANES, stride=2), :].astype(jnp.bfloat16)
                wu[at, at_cols] = pairs[n, pl.ds(1, LANES, stride=2), :].astype(jnp.bfloat16)
            return carry

        lax.fori_loop(0, cols // (2 * LANES), body, 0)
        if ct + 2 < hidden // LANES:
            stage_copy(ct + 2).start()

    def exchange(s, first_slot, count, j):
        at = pl.ds(first_slot * rows, count * rows)
        return remote(sent.at[j, :, at], got.at[j, :, at], p_send.at[s, j], p_recv.at[s, j],
                      me, 1 - core)

    def project_in(s, first_slot, count):
        size = count * rows
        block = pl.ds(first_slot, count)
        at_rows = pl.ds(first_slot * rows, size)

        def body(j, carry):
            at = pl.ds(pl.multiple_of(j * TILE, TILE), TILE)
            value = xs[block, :, :cols].reshape(size, cols)
            gate = jnp.dot(value, wg[:, at], preferred_element_type=jnp.float32)
            up = jnp.dot(value, wu[:, at], preferred_element_type=jnp.float32)
            part[j, 0, :size] = gate
            part[j, 1, :size] = up
            for k, value in ((0, gate), (1, up)):
                value = value.astype(jnp.bfloat16)
                for n in range(count):
                    theirs = pl.ds(twin_of(first_slot + n) * rows, rows)
                    sent[j, k, theirs] = value[n * rows:(n + 1) * rows]
            exchange(s, first_slot, count, j).start()
            return carry

        lax.fori_loop(0, tiles, body, 0)

    def activate(s, first_slot, count):
        size = count * rows
        at_rows = pl.ds(first_slot * rows, size)

        def body(j, carry):
            exchange(s, first_slot, count, j).wait_recv()
            gate = part[j, 0, :size] + got[j, 0, at_rows].astype(jnp.float32)
            up = part[j, 1, :size] + got[j, 1, at_rows].astype(jnp.float32)
            act[:size, pl.ds(pl.multiple_of(j * TILE, TILE), TILE)] = (
                gate / (1.0 + jnp.exp(-gate)) * up
            ).astype(jnp.bfloat16)
            return carry

        lax.fori_loop(0, tiles, body, 0)

    wide_tiles = cols // WIDE_TILE
    per_piece = -(-wide_tiles // PIECES)
    bounds = [min(n * per_piece, wide_tiles) for n in range(PIECES + 1)]
    every_piece = [h for h in range(PIECES) if bounds[h] < bounds[h + 1]]

    def cut(h):
        return pl.ds(bounds[h] * WIDE_TILE, (bounds[h + 1] - bounds[h]) * WIDE_TILE)

    def project_out(first_slot, count, h):
        size = count * rows
        block = pl.ds(first_slot, count)
        lane = lax.broadcasted_iota(jnp.int32, (size, LANES), 1)
        mine = (lane % 16 == me) & (lane < 48)
        scales = xs[block, :, cols:].reshape(size, LANES).astype(jnp.float32)
        scale = jnp.sum(jnp.where(mine, scales, 0.0), axis=1, keepdims=True)

        def body(j, carry):
            at = pl.ds(pl.multiple_of(j * WIDE_TILE, WIDE_TILE), WIDE_TILE)
            value = jnp.dot(act[:size], wo[:, at], preferred_element_type=jnp.float32)
            value = value * scale
            contrib[block, :, at] = value.astype(jnp.bfloat16).reshape(count, rows, WIDE_TILE)
            return carry

        lax.fori_loop(bounds[h], bounds[h + 1], body, 0)

    def add_up(h, target, terms):
        def body(j, carry):
            at = pl.ds(pl.multiple_of(j * WIDE_TILE, WIDE_TILE), WIDE_TILE)
            total = terms[0][:, at].astype(jnp.float32)
            for term in terms[1:]:
                total = total + term[:, at].astype(jnp.float32)
            target[:, at] = total.astype(jnp.bfloat16)
            return carry

        lax.fori_loop(bounds[h], bounds[h + 1], body, 0)

    def pass_sum(plane, h, slot, target, send, recv, chip):
        start(plane, lambda: remote(
            contrib.at[slot, :, cut(h)], target[0].at[target[1]].at[:, cut(h)],
            send.at[(*target[1], h)], recv.at[(*target[1], h)], chip))

    def cross(rank, h):
        pass_sum("all", h, slot_of(SIDE_B, rank), (a_in, (rank,)), a_send, a_recv, near_a)
        pass_sum("all", h, slot_of(SIDE_A, rank), (b_in, (rank,)), b_send, b_recv, near_b)

    def straight(h):
        pass_sum("all", h, slot_of(SIDE_B, 0), (b_in, (0,)), b_send, b_recv, near_b)

    sends["all"] = []

    def take(buffer, recv, index, h):
        arrived(buffer.at[(*index, slice(None), cut(h))], recv.at[(*index, h)])
        return buffer.at[index]

    def along(line, rank, h):
        kind = line // DIAGONAL

        def act_on(plane):
            there = NEAREST[plane][rank]
            way = UP if there > plane else DOWN
            far = abs(there - plane)
            slot = slot_of(line, rank)
            terms = [contrib.at[slot]]
            if line == DIAGONAL:
                terms.append(take(a_in, a_recv, (rank,), h))
                terms.append(take(b_in, b_recv, (rank,), h))
            if plane != (0 if way == UP else LINE - 1):
                terms.append(take(z_in, z_recv, (kind, way, far), h))
            if len(terms) > 1:
                add_up(h, contrib.at[slot], terms)
            pass_sum(plane, h, slot, (z_in, (kind, way, far - 1)), z_send, z_recv,
                     chips[TO_UP if way == UP else TO_DOWN])
        return act_on

    def from_line(plane, kind, h):
        return [
            take(z_in, z_recv, (kind, way, 0), h)
            for way, stop in ((UP, 0), (DOWN, LINE - 1)) if plane != stop
        ]

    def turn_b(h):
        def act_on(plane):
            slot = slot_of(DIAGONAL, 0)
            add_up(h, contrib.at[slot], [contrib.at[slot], *from_line(plane, 1, h)])
            pass_sum(plane, h, slot, (b_in, (LINE,)), b_send, b_recv, near_b)
        return act_on

    def turn_a(h):
        slot = slot_of(SIDE_A, 0)
        add_up(h, contrib.at[slot], [contrib.at[slot], take(b_in, b_recv, (LINE,), h)])
        pass_sum("all", h, slot, (a_in, (0,)), a_send, a_recv, near_a)

    def finish(h):
        def act_on(plane):
            terms = [contrib.at[0], take(b_in, b_recv, (0,), h), *from_line(plane, 0, h)]
            add_up(h, out_ref, [*terms, take(a_in, a_recv, (0,), h)])
        return act_on

    def feed(s):
        project_in(s, *groups[s])

    def blend(s):
        activate(s, *groups[s])

    def close(s, h):
        project_out(*groups[s], h)

    on(EVERY, send_own)
    tiles_in = hidden // LANES
    stage_copy(0).start()
    stage_copy(1).start()
    out_weights = pltpu.make_async_copy(w_out_ref.at[0], wo, wo_sem)
    out_weights.start()
    xs[0] = ext_ref[...]
    groups = ((0, 2), (2, 2), (4, 4), (8, 2), (10, 2), (12, 4))
    for ct in range(tiles_in // 2):
        sort_tile(ct)
    on(EVERY, relay_side(0))
    on(EVERY, pass_z(1, 0))
    on(INNER, pass_z(2, 0))
    for ct in range(tiles_in // 2, tiles_in):
        sort_tile(ct)
    on(EVERY, relay_side(1))
    on(EVERY, pass_z(1, 1))
    on(EVERY, pass_ab(1, 0))
    on(EVERY, pass_ab(1, 1))
    on(INNER, pass_z(2, 1))
    on(INNER, pass_ab(2, 0))
    on(INNER, pass_ab(2, 1))
    feed(0)
    on(INNER, pass_z(3, 0))
    on(ENDS, relay_own(2, 0))
    on(EVERY, relay_diagonal(0, 0))
    blend(0)
    out_weights.wait()
    for h in every_piece:
        close(0, h)
    on(INNER, pass_z(3, 1))
    on(INNER, pass_ab(3, 0))
    on(INNER, pass_ab(3, 1))
    on(ENDS, relay_own(2, 1))
    on(EVERY, relay_diagonal(0, 1))
    for h in every_piece:
        on(ENDS, along(OWN, 1, h))
    wait_for(SIDE_B, 0)
    feed(1)
    on(INNER, relay_diagonal(1, 0))
    on(ENDS, relay_own(3, 0))
    blend(1)
    for h in every_piece:
        close(1, h)
        straight(h)
    on(ENDS, relay_own(3, 1))
    on(INNER, relay_diagonal(1, 1))
    on(INNER, relay_diagonal(2, 0))
    wait_for(SIDE_A, 1)
    wait_for(SIDE_B, 1)
    feed(2)
    on(INNER, relay_diagonal(2, 1))
    on(INNER, relay_diagonal(3, 0))
    blend(2)
    for h in every_piece:
        close(2, h)
        cross(1, h)
        on(ENDS, along(OWN, 3, h))
        on(ENDS, along(OWN, 2, h))
    on(INNER, relay_diagonal(3, 1))
    wait_for(SIDE_A, 2)
    wait_for(SIDE_B, 2)
    feed(3)
    blend(3)
    for h in every_piece:
        close(3, h)
    wait_for(SIDE_A, 3)
    wait_for(SIDE_B, 3)
    feed(4)
    for h in every_piece[:PIECES // 2]:
        on(INNER, along(OWN, 3, h))
    blend(4)
    for h in every_piece[PIECES // 2:]:
        on(INNER, along(OWN, 3, h))
    for h in every_piece:
        close(4, h)
        cross(3, h)
    for h in every_piece:
        cross(2, h)
    for rank in (1, 2, 3):
        on(ENDS, lambda plane: wait_for(DIAGONAL, rank))
    feed(5)
    for h in every_piece:
        on(INNER, along(OWN, 2, h))
        on(INNER, along(OWN, 1, h))
    blend(5)
    for h in every_piece:
        close(5, h)
        on(ENDS, along(DIAGONAL, 3, h))
    for h in every_piece:
        on(INNER, along(DIAGONAL, 3, h))
    for h in every_piece:
        on(ENDS, along(DIAGONAL, 2, h))
        on(INNER, along(DIAGONAL, 1, h))
    for h in every_piece:
        on(ENDS, along(DIAGONAL, 1, h))
        on(INNER, along(DIAGONAL, 2, h))
    for h in every_piece:
        on(EVERY, turn_b(h))
    for h in every_piece:
        turn_a(h)
    for h in every_piece:
        on(EVERY, finish(h))
    for copy in sends["all"]:
        copy().wait_send()

    def drained(plane):
        for copy in sends[plane]:
            copy().wait_send()

    on(EVERY, drained)
    for s, (first_slot, count) in enumerate(groups):
        def drain(j, carry):
            exchange(s, first_slot, count, j).wait_send()
            return carry

        lax.fori_loop(0, tiles, drain, 0)


def fused(tokens, routes, route_scores, placement, w_in, w_out):
    rows, cols = tokens.shape
    hidden = w_in.shape[3]
    tiles = hidden // TILE
    table = expert_weights(routes, route_scores, placement)
    high = lax.reduce_precision(table, 8, 7)
    middle = lax.reduce_precision(table - high, 8, 7)
    low = table - high - middle
    thirds = [third.astype(jnp.bfloat16) for third in (high, middle, low)]
    filler = jnp.zeros((rows, LANES - 3 * table.shape[1]), jnp.bfloat16)
    ext = jnp.concatenate([tokens, *thirds, filler], axis=1)
    slots = LINE * LINE
    bf16 = jnp.bfloat16
    dma = pltpu.SemaphoreType.DMA
    return pl.pallas_call(
        layer_kernel,
        out_shape=jax.ShapeDtypeStruct((rows, cols), bf16),
        in_specs=[
            pl.BlockSpec(memory_space=pltpu.VMEM),
            pl.BlockSpec(memory_space=pl.ANY),
            pl.BlockSpec(memory_space=pl.ANY),
        ],
        out_specs=pl.BlockSpec(memory_space=pltpu.VMEM),
        scratch_shapes=[
            pltpu.VMEM((slots, rows, cols + LANES), bf16),
            pltpu.VMEM((cols, hidden), bf16),
            pltpu.VMEM((cols, hidden), bf16),
            pltpu.VMEM((2, cols, 2, LANES), bf16),
            pltpu.VMEM((2, 2 * LANES, LANES), jnp.float32),
            pltpu.VMEM((hidden, cols), bf16),
            pltpu.VMEM((slots, rows, cols), bf16),
            pltpu.VMEM((2, 2, LINE - 1, rows, cols), bf16),
            pltpu.VMEM((LINE, rows, cols), bf16),
            pltpu.VMEM((LINE + 1, rows, cols), bf16),
            pltpu.VMEM((tiles, 2, LINE * rows, TILE), jnp.float32),
            pltpu.VMEM((tiles, 2, slots * rows, TILE), bf16),
            pltpu.VMEM((tiles, 2, slots * rows, TILE), bf16),
            pltpu.VMEM((LINE * rows, hidden), bf16),
            dma((2,)), dma, dma((4, slots, 2)), dma((slots, 2)),
            dma((slots, tiles)), dma((slots, tiles)),
            dma((2, 2, LINE - 1, PIECES)), dma((2, 2, LINE - 1, PIECES)),
            dma((LINE, PIECES)), dma((LINE, PIECES)),
            dma((LINE + 1, PIECES)), dma((LINE + 1, PIECES)),
        ],
        compiler_params=pltpu.CompilerParams(
            collective_id=0, has_side_effects=True, vmem_limit_bytes=67043328
        ),
    )(ext, w_in, w_out)


def on_device(tokens, routes, route_scores, placement, w_in, w_out):
    tok_rows = tokens.shape[0]
    experts = placement.shape[0]
    fits = experts == 4 * LINE and lax.axis_size("replica") == 2
    if fits and 2 * tok_rows * routes.shape[1] // experts >= tok_rows:
        return fused(tokens, routes, route_scores, placement, w_in, w_out)
    return packed(tokens, routes, route_scores, placement, w_in, w_out)


def solution(mesh):
    in_specs = (
        P("expert", "replica"),
        P("expert", None),
        P("expert", None),
        P(),
        P("expert", "replica", None, None),
        P("expert", None, "replica"),
    )
    out_specs = P("expert", "replica")
    return jax.shard_map(
        on_device, mesh=mesh, in_specs=in_specs, out_specs=out_specs, check_vma=False
    )
```

```python
import functools

import jax
import jax.numpy as jnp
from jax import lax
from jax.experimental import pallas as pl
from jax.experimental.pallas import tpu as pltpu
from jax.sharding import PartitionSpec as P

LANES = 128
TILE = 256
WIDE_TILE = 512
PIECES = 4
DEPTH = 3
MESH = pl.DeviceIdType.MESH
LINE = 4
OWN, SIDE_A, SIDE_B, DIAGONAL = range(4)
UP, DOWN = range(2)
TO_A, TO_B, TO_UP, TO_DOWN = range(4)
NEAREST = ((0, 1, 2, 3), (1, 0, 2, 3), (2, 3, 1, 0), (3, 2, 1, 0))
ENDS, INNER, EVERY = (0, LINE - 1), (1, 2), (0, 1, 2, 3)
SLOTS = (
    (OWN, 0), (OWN, 1), (SIDE_A, 0), (SIDE_B, 0), (OWN, 2), (OWN, 3), (SIDE_A, 1), (SIDE_B, 1),
    (SIDE_A, 2), (SIDE_B, 2), (SIDE_A, 3), (SIDE_B, 3),
    (DIAGONAL, 0), (DIAGONAL, 1), (DIAGONAL, 2), (DIAGONAL, 3),
)


def slot_of(line, rank):
    return SLOTS.index((line, rank))


def twin_of(slot):
    line, rank = SLOTS[slot]
    return slot_of({SIDE_A: SIDE_B, SIDE_B: SIDE_A}.get(line, line), rank)


def packed(tokens, routes, route_scores, placement, w_in, w_out):
    tok_rows, feature_cols = tokens.shape
    route_count = routes.shape[1]
    experts = placement.shape[0]
    hidden_units = w_in.shape[3]
    capacity = min(tok_rows, max(2, 2 * tok_rows * route_count // experts))
    slot_total = experts * capacity
    expert_ids = jnp.arange(experts, dtype=jnp.int32)
    route_table = routes[:, :, None] == expert_ids
    physical = jnp.sum(jnp.where(route_table, placement, 0), axis=-1)
    flat_slots = physical.reshape(-1)
    onehot = (flat_slots[:, None] == expert_ids).astype(jnp.int32)
    earlier = jnp.sum((jnp.cumsum(onehot, axis=0) - onehot) * onehot, axis=1)
    position = (flat_slots * capacity + earlier).reshape(tok_rows, route_count)
    slot_index = jnp.arange(slot_total, dtype=jnp.int32)
    placing = jnp.any(position[None, :, :] == slot_index[:, None, None], axis=-1).astype(
        jnp.bfloat16
    )
    outgoing = jnp.dot(placing, tokens, preferred_element_type=jnp.float32).astype(jnp.bfloat16)
    incoming = lax.all_to_all(outgoing, "expert", split_axis=0, concat_axis=0, tiled=True)
    weights_in = w_in[0].reshape(feature_cols, 2 * hidden_units)
    weights_out = w_out[0]
    partial_value = jnp.dot(incoming, weights_in, preferred_element_type=jnp.float32)
    partial_value = partial_value.reshape(slot_total, 2, hidden_units)
    shares = lax.psum_scatter(partial_value, "replica", scatter_dimension=2, tiled=True)
    active = (jax.nn.silu(shares[:, 0]) * shares[:, 1]).astype(jnp.bfloat16)
    result = jnp.dot(
        lax.all_gather(active, "replica", axis=1, tiled=True),
        weights_out,
        preferred_element_type=jnp.float32,
    )
    expert_out = result.astype(jnp.bfloat16)
    returned = lax.all_to_all(expert_out, "expert", split_axis=0, concat_axis=0, tiled=True)
    route_weight = 2.5 * route_scores / jnp.sum(route_scores, axis=1, keepdims=True)
    picked = returned[position.reshape(-1)].reshape(tok_rows, route_count, feature_cols)
    mixed = jnp.sum(picked.astype(jnp.float32) * route_weight[:, :, None], axis=1)
    return mixed.astype(jnp.bfloat16)


def weight_columns(routes_ref, scores_ref, placement_ref):
    routes = routes_ref[...]
    scores = scores_ref[...]
    experts = placement_ref.shape[0]
    physical = jnp.zeros_like(routes)
    for expert in range(experts):
        physical = jnp.where(routes == expert, placement_ref[expert], physical)
    route_weight = 2.5 * scores / jnp.sum(scores, axis=0, keepdims=True)
    column = lax.broadcasted_iota(jnp.int32, (LANES, routes.shape[1]), 0)
    table = jnp.zeros(column.shape, jnp.float32)
    for k in range(routes.shape[0]):
        chosen = physical[k:k + 1, :] == column % experts
        table = jnp.where(chosen, route_weight[k:k + 1, :], table)
    high = table.astype(jnp.bfloat16).astype(jnp.float32)
    middle = (table - high).astype(jnp.bfloat16).astype(jnp.float32)
    low = table - high - middle
    thirds = jnp.where(column < experts, high, jnp.where(column < 2 * experts, middle, low))
    return jnp.where(column < 3 * experts, thirds, 0.0).T.astype(jnp.bfloat16)


def layer_kernel(
    tokens_ref, routes_ref, scores_ref, placement_ref, w_in_ref, w_out_ref, out_ref,
    xs, wg, wu, stage, pairs, wo, contrib, z_in, a_in, b_in, part, sent, got, act,
    t_sem, w_sem, wo_sem, x_send, x_recv, p_send, p_recv,
    z_send, z_recv, a_send, a_recv, b_send, b_recv,
):
    rows, cols = out_ref.shape
    hidden = wg.shape[1]
    own_tokens = pltpu.make_async_copy(tokens_ref, xs.at[0, :, :cols], t_sem)
    own_tokens.start()
    out_weights = pltpu.make_async_copy(w_out_ref.at[0], wo, wo_sem)

    def stage_copy(ct):
        return pltpu.make_async_copy(
            w_in_ref.at[0].reshape(2 * cols, hidden).at[:, pl.ds(ct * LANES, LANES)],
            stage.at[ct % DEPTH], w_sem.at[ct % DEPTH]
        )

    for ct in range(DEPTH):
        stage_copy(ct).start()
    xs[0, :, cols:] = weight_columns(routes_ref, scores_ref, placement_ref)
    tiles = hidden // TILE
    me = lax.axis_index("expert")
    core = lax.axis_index("replica")
    x, y, z = me % 2, (me // 2) % 2, me // 4
    flip_x, flip_y = me + 1 - 2 * x, me + 2 - 4 * y
    near_a = (1 - core) * flip_x + core * flip_y
    near_b = (1 - core) * flip_y + core * flip_x
    chips = (near_a, near_b, me + 4, me - 4)
    sends = {plane: [] for plane in EVERY}

    def on(planes, act_on):
        for plane in planes:
            pl.when(z == plane)(functools.partial(act_on, plane))

    def remote(src, dst, send, recv, chip, on_core=None):
        return pltpu.make_async_remote_copy(
            src_ref=src, dst_ref=dst, send_sem=send, recv_sem=recv,
            device_id=(chip, core if on_core is None else on_core), device_id_type=MESH,
        )

    def arrived(ref, recv):
        remote(ref, ref, a_send.at[0, 0], recv, near_a).wait_recv()

    barrier = pltpu.get_barrier_semaphore()
    for peer in ((near_a, core), (near_b, core), (me, 1 - core)):
        pl.semaphore_signal(barrier, inc=1, device_id=peer, device_id_type=MESH)

    def greet(plane):
        for step, there in ((4, plane + 1), (-4, plane - 1)):
            if 0 <= there < LINE:
                pl.semaphore_signal(
                    barrier, inc=1, device_id=(me + step, core), device_id_type=MESH
                )
        pl.semaphore_wait(barrier, 4 if plane in ENDS else 5)

    on(EVERY, greet)

    def start(plane, copy):
        copy().start()
        sends[plane].append(copy)

    part_rows = rows // 2

    def piece(h):
        return pl.ds(h * part_rows, part_rows)

    def ship(plane, source, from_slot, to_slot, kind, h):
        start(plane, lambda: remote(
            source(), xs.at[to_slot, piece(h)], x_send.at[kind, from_slot, h],
            x_recv.at[to_slot, h], chips[kind]))

    def landed(slot, h):
        arrived(xs.at[slot, piece(h)], x_recv.at[slot, h])
        return lambda: xs.at[slot, piece(h)]

    def ship_along(plane, source, line, rank, h):
        there = NEAREST[plane][rank]
        slot = slot_of(line, rank)
        if plane < LINE - 1 and there <= plane:
            ship(plane, source, slot, slot_of(line, NEAREST[plane + 1].index(there)), TO_UP, h)
        if plane > 0 and there >= plane:
            ship(plane, source, slot, slot_of(line, NEAREST[plane - 1].index(there)), TO_DOWN, h)

    def own_piece(h):
        return xs.at[0, piece(h)]

    def send_own(plane):
        for h in range(2):
            source = functools.partial(own_piece, h)
            ship(plane, source, 0, slot_of(SIDE_A, 0), TO_A, h)
            ship(plane, source, 0, slot_of(SIDE_B, 0), TO_B, h)
            ship_along(plane, source, OWN, 0, h)

    def relay_own(rank, h):
        def act_on(plane):
            slot = slot_of(OWN, rank)
            source = landed(slot, h)
            ship_along(plane, source, OWN, rank, h)
            ship(plane, source, slot, slot_of(SIDE_A, rank), TO_A, h)
            ship(plane, source, slot, slot_of(SIDE_B, rank), TO_B, h)
        return act_on

    def pass_z(rank, h):
        def act_on(plane):
            ship_along(plane, landed(slot_of(OWN, rank), h), OWN, rank, h)
        return act_on

    def pass_ab(rank, h):
        def act_on(plane):
            slot = slot_of(OWN, rank)

            def held():
                return xs.at[slot, piece(h)]

            ship(plane, held, slot, slot_of(SIDE_A, rank), TO_A, h)
            ship(plane, held, slot, slot_of(SIDE_B, rank), TO_B, h)
        return act_on

    def relay_side(h):
        def act_on(plane):
            slot = slot_of(SIDE_A, 0)
            ship(plane, landed(slot, h), slot, slot_of(DIAGONAL, 0), TO_B, h)
        return act_on

    def relay_diagonal(rank, h):
        def act_on(plane):
            ship_along(plane, landed(slot_of(DIAGONAL, rank), h), DIAGONAL, rank, h)
        return act_on

    def wait_for(line, rank):
        for h in range(2):
            landed(slot_of(line, rank), h)

    def sort_tile(ct):
        stage_copy(ct).wait()
        at_cols = slice(ct * LANES, (ct + 1) * LANES)

        flat = stage.at[ct % DEPTH]

        def body(k, carry):
            for n in range(2):
                first = pl.multiple_of((2 * k + n) * LANES, LANES)
                at = pl.ds(first, LANES)
                pairs[n] = flat[pl.ds(2 * first, 2 * LANES), :].astype(jnp.float32)
                wg[at, at_cols] = pairs[n, pl.ds(0, LANES, stride=2), :].astype(jnp.bfloat16)
                wu[at, at_cols] = pairs[n, pl.ds(1, LANES, stride=2), :].astype(jnp.bfloat16)
            return carry

        lax.fori_loop(0, cols // (2 * LANES), body, 0)
        if ct + DEPTH < hidden // LANES:
            stage_copy(ct + DEPTH).start()
        if ct + DEPTH == hidden // LANES:
            out_weights.start()

    def exchange(s, first_slot, count, j):
        at = pl.ds(first_slot * rows, count * rows)
        return remote(sent.at[j, :, at], got.at[j, :, at], p_send.at[s, j], p_recv.at[s, j],
                      me, 1 - core)

    def project_in(s, first_slot, count, j):
        size = count * rows
        at = pl.ds(j * TILE if isinstance(j, int) else pl.multiple_of(j * TILE, TILE), TILE)
        value = xs[pl.ds(first_slot, count), :, :cols].reshape(size, cols)
        for k, weights in ((0, wg), (1, wu)):
            total = jnp.dot(value, weights[:, at], preferred_element_type=jnp.float32)
            part[j, k, :size] = total
            total = total.astype(jnp.bfloat16)
            for n in range(count):
                theirs = pl.ds(twin_of(first_slot + n) * rows, rows)
                sent[j, k, theirs] = total[n * rows:(n + 1) * rows]
        exchange(s, first_slot, count, j).start()

    def activate(first_slot, count, j):
        size = count * rows
        at_rows = pl.ds(first_slot * rows, size)
        gate = part[j, 0, :size] + got[j, 0, at_rows].astype(jnp.float32)
        up = part[j, 1, :size] + got[j, 1, at_rows].astype(jnp.float32)
        at = pl.ds(j * TILE if isinstance(j, int) else pl.multiple_of(j * TILE, TILE), TILE)
        act[:size, at] = (gate / (1.0 + jnp.exp(-gate)) * up).astype(jnp.bfloat16)

    wide_tiles = cols // WIDE_TILE
    per_piece = -(-wide_tiles // PIECES)
    bounds = [min(n * per_piece, wide_tiles) for n in range(PIECES + 1)]
    every_piece = [h for h in range(PIECES) if bounds[h] < bounds[h + 1]]

    def cut(h):
        return pl.ds(bounds[h] * WIDE_TILE, (bounds[h + 1] - bounds[h]) * WIDE_TILE)

    def project_out(first_slot, count, h):
        size = count * rows
        block = pl.ds(first_slot, count)
        lane = lax.broadcasted_iota(jnp.int32, (size, LANES), 1)
        mine = (lane % 16 == me) & (lane < 48)
        scales = xs[block, :, cols:].reshape(size, LANES).astype(jnp.float32)
        scale = jnp.sum(jnp.where(mine, scales, 0.0), axis=1, keepdims=True)

        def body(j, carry):
            at = pl.ds(pl.multiple_of(j * WIDE_TILE, WIDE_TILE), WIDE_TILE)
            value = jnp.dot(act[:size], wo[:, at], preferred_element_type=jnp.float32)
            value = value * scale
            contrib[block, :, at] = value.astype(jnp.bfloat16).reshape(count, rows, WIDE_TILE)
            return carry

        lax.fori_loop(bounds[h], bounds[h + 1], body, 0)

    def add_up(h, target, terms):
        def body(j, carry):
            at = pl.ds(pl.multiple_of(j * WIDE_TILE, WIDE_TILE), WIDE_TILE)
            total = terms[0][:, at].astype(jnp.float32)
            for term in terms[1:]:
                total = total + term[:, at].astype(jnp.float32)
            target[:, at] = total.astype(jnp.bfloat16)
            return carry

        lax.fori_loop(bounds[h], bounds[h + 1], body, 0)

    def pass_sum(plane, h, slot, target, send, recv, chip):
        start(plane, lambda: remote(
            contrib.at[slot, :, cut(h)], target[0].at[target[1]].at[:, cut(h)],
            send.at[(*target[1], h)], recv.at[(*target[1], h)], chip))

    def cross(rank, h):
        pass_sum("all", h, slot_of(SIDE_B, rank), (a_in, (rank,)), a_send, a_recv, near_a)
        pass_sum("all", h, slot_of(SIDE_A, rank), (b_in, (rank,)), b_send, b_recv, near_b)

    def straight(h):
        pass_sum("all", h, slot_of(SIDE_B, 0), (b_in, (0,)), b_send, b_recv, near_b)

    sends["all"] = []

    def take(buffer, recv, index, h):
        arrived(buffer.at[(*index, slice(None), cut(h))], recv.at[(*index, h)])
        return buffer.at[index]

    def along(line, rank, h):
        kind = line // DIAGONAL

        def act_on(plane):
            there = NEAREST[plane][rank]
            way = UP if there > plane else DOWN
            far = abs(there - plane)
            slot = slot_of(line, rank)
            terms = [contrib.at[slot]]
            if line == DIAGONAL:
                terms.append(take(a_in, a_recv, (rank,), h))
                terms.append(take(b_in, b_recv, (rank,), h))
            if plane != (0 if way == UP else LINE - 1):
                terms.append(take(z_in, z_recv, (kind, way, far), h))
            if len(terms) > 1:
                add_up(h, contrib.at[slot], terms)
            pass_sum(plane, h, slot, (z_in, (kind, way, far - 1)), z_send, z_recv,
                     chips[TO_UP if way == UP else TO_DOWN])
        return act_on

    def from_line(plane, kind, h):
        return [
            take(z_in, z_recv, (kind, way, 0), h)
            for way, stop in ((UP, 0), (DOWN, LINE - 1)) if plane != stop
        ]

    def turn_b(h):
        def act_on(plane):
            slot = slot_of(DIAGONAL, 0)
            add_up(h, contrib.at[slot], [contrib.at[slot], *from_line(plane, 1, h)])
            pass_sum(plane, h, slot, (b_in, (LINE,)), b_send, b_recv, near_b)
        return act_on

    def turn_a(h):
        slot = slot_of(SIDE_A, 0)
        add_up(h, contrib.at[slot], [contrib.at[slot], take(b_in, b_recv, (LINE,), h)])
        pass_sum("all", h, slot, (a_in, (0,)), a_send, a_recv, near_a)

    def finish(h):
        def act_on(plane):
            terms = [contrib.at[0], take(b_in, b_recv, (0,), h), *from_line(plane, 0, h)]
            add_up(h, out_ref, [*terms, take(a_in, a_recv, (0,), h)])
        return act_on

    def feed(s):
        def body(j, carry):
            project_in(s, *groups[s], j)
            return carry

        lax.fori_loop(0, tiles, body, 0)

    def blend(s):
        def body(j, carry):
            exchange(s, *groups[s], j).wait_recv()
            activate(*groups[s], j)
            return carry

        lax.fori_loop(0, tiles, body, 0)

    def close(s, h):
        project_out(*groups[s], h)

    own_tokens.wait()
    on(EVERY, send_own)
    tiles_in = hidden // LANES
    groups = ((0, 2), (2, 2), (4, 4), (8, 2), (10, 2), (12, 4))
    for ct in range(tiles_in // 2):
        sort_tile(ct)
    on(EVERY, relay_side(0))
    on(EVERY, pass_z(1, 0))
    on(INNER, pass_z(2, 0))
    for ct in range(tiles_in // 2, tiles_in):
        sort_tile(ct)
    on(EVERY, relay_side(1))
    on(EVERY, pass_z(1, 1))
    on(EVERY, pass_ab(1, 0))
    on(EVERY, pass_ab(1, 1))
    on(INNER, pass_z(2, 1))
    on(INNER, pass_ab(2, 0))
    on(INNER, pass_ab(2, 1))
    feed(0)
    on(INNER, pass_z(3, 0))
    on(ENDS, relay_own(2, 0))
    on(EVERY, relay_diagonal(0, 0))
    blend(0)
    out_weights.wait()
    for h in every_piece:
        close(0, h)
    on(INNER, pass_z(3, 1))
    on(INNER, pass_ab(3, 0))
    on(INNER, pass_ab(3, 1))
    on(ENDS, relay_own(2, 1))
    on(EVERY, relay_diagonal(0, 1))
    for h in every_piece:
        on(ENDS, along(OWN, 1, h))
    wait_for(SIDE_B, 0)
    feed(1)
    on(INNER, relay_diagonal(1, 0))
    on(ENDS, relay_own(3, 0))
    blend(1)
    for h in every_piece:
        close(1, h)
        straight(h)
    on(ENDS, relay_own(3, 1))
    on(INNER, relay_diagonal(1, 1))
    on(INNER, relay_diagonal(2, 0))
    wait_for(SIDE_A, 1)
    wait_for(SIDE_B, 1)
    feed(2)
    on(INNER, relay_diagonal(2, 1))
    on(INNER, relay_diagonal(3, 0))
    blend(2)
    for h in every_piece:
        close(2, h)
        cross(1, h)
        on(ENDS, along(OWN, 3, h))
        on(ENDS, along(OWN, 2, h))
    on(INNER, relay_diagonal(3, 1))
    wait_for(SIDE_A, 2)
    wait_for(SIDE_B, 2)
    feed(3)
    blend(3)
    for h in every_piece:
        close(3, h)
    wait_for(SIDE_A, 3)
    wait_for(SIDE_B, 3)
    feed(4)
    for h in every_piece[:PIECES // 2]:
        on(INNER, along(OWN, 3, h))
    blend(4)
    for h in every_piece[PIECES // 2:]:
        on(INNER, along(OWN, 3, h))
    for h in every_piece:
        close(4, h)
        cross(3, h)
    for h in every_piece:
        cross(2, h)
    for rank in (1, 2, 3):
        on(ENDS, lambda plane: wait_for(DIAGONAL, rank))
    feed(5)
    for h in every_piece:
        on(INNER, along(OWN, 2, h))
        on(INNER, along(OWN, 1, h))
    blend(5)
    for h in every_piece:
        close(5, h)
        on(ENDS, along(DIAGONAL, 3, h))
    for h in every_piece:
        on(INNER, along(DIAGONAL, 3, h))
    for h in every_piece:
        on(ENDS, along(DIAGONAL, 2, h))
        on(INNER, along(DIAGONAL, 1, h))
    for h in every_piece:
        on(ENDS, along(DIAGONAL, 1, h))
        on(INNER, along(DIAGONAL, 2, h))
    for h in every_piece:
        on(EVERY, turn_b(h))
    for h in every_piece:
        turn_a(h)
    for h in every_piece:
        on(EVERY, finish(h))
    for copy in sends["all"]:
        copy().wait_send()

    def drained(plane):
        for copy in sends[plane]:
            copy().wait_send()

    on(EVERY, drained)
    for s, (first_slot, count) in enumerate(groups):
        def drain(j, carry):
            exchange(s, first_slot, count, j).wait_send()
            return carry

        lax.fori_loop(0, tiles, drain, 0)


def fused(tokens, routes, route_scores, placement, w_in, w_out):
    rows, cols = tokens.shape
    hidden = w_in.shape[3]
    tiles = hidden // TILE
    slots = LINE * LINE
    bf16 = jnp.bfloat16
    dma = pltpu.SemaphoreType.DMA
    return pl.pallas_call(
        layer_kernel,
        out_shape=jax.ShapeDtypeStruct((rows, cols), bf16),
        in_specs=[
            pl.BlockSpec(memory_space=pl.ANY),
            pl.BlockSpec(memory_space=pltpu.VMEM),
            pl.BlockSpec(memory_space=pltpu.VMEM),
            pl.BlockSpec(memory_space=pltpu.SMEM),
            pl.BlockSpec(memory_space=pl.ANY),
            pl.BlockSpec(memory_space=pl.ANY),
        ],
        out_specs=pl.BlockSpec(memory_space=pltpu.VMEM),
        scratch_shapes=[
            pltpu.VMEM((slots, rows, cols + LANES), bf16),
            pltpu.VMEM((cols, hidden), bf16),
            pltpu.VMEM((cols, hidden), bf16),
            pltpu.VMEM((DEPTH, 2 * cols, LANES), bf16),
            pltpu.VMEM((2, 2 * LANES, LANES), jnp.float32),
            pltpu.VMEM((hidden, cols), bf16),
            pltpu.VMEM((slots, rows, cols), bf16),
            pltpu.VMEM((2, 2, LINE - 1, rows, cols), bf16),
            pltpu.VMEM((LINE, rows, cols), bf16),
            pltpu.VMEM((LINE + 1, rows, cols), bf16),
            pltpu.VMEM((tiles, 2, LINE * rows, TILE), jnp.float32),
            pltpu.VMEM((tiles, 2, slots * rows, TILE), bf16),
            pltpu.VMEM((tiles, 2, slots * rows, TILE), bf16),
            pltpu.VMEM((LINE * rows, hidden), bf16),
            dma, dma((DEPTH,)), dma, dma((4, slots, 2)), dma((slots, 2)),
            dma((slots, tiles)), dma((slots, tiles)),
            dma((2, 2, LINE - 1, PIECES)), dma((2, 2, LINE - 1, PIECES)),
            dma((LINE, PIECES)), dma((LINE, PIECES)),
            dma((LINE + 1, PIECES)), dma((LINE + 1, PIECES)),
        ],
        compiler_params=pltpu.CompilerParams(
            collective_id=0, has_side_effects=True, vmem_limit_bytes=67043328
        ),
    )(tokens, routes.T, route_scores.T, placement, w_in, w_out)


def on_device(tokens, routes, route_scores, placement, w_in, w_out):
    tok_rows = tokens.shape[0]
    experts = placement.shape[0]
    fits = experts == 4 * LINE and lax.axis_size("replica") == 2
    if fits and 2 * tok_rows * routes.shape[1] // experts >= tok_rows:
        return fused(tokens, routes, route_scores, placement, w_in, w_out)
    return packed(tokens, routes, route_scores, placement, w_in, w_out)


def solution(mesh):
    in_specs = (
        P("expert", "replica"),
        P("expert", None),
        P("expert", None),
        P(),
        P("expert", "replica", None, None),
        P("expert", None, "replica"),
    )
    out_specs = P("expert", "replica")
    return jax.shard_map(
        on_device, mesh=mesh, in_specs=in_specs, out_specs=out_specs, check_vma=False
    )
```

```python
import functools

import jax
import jax.numpy as jnp
from jax import lax
from jax.experimental import pallas as pl
from jax.experimental.pallas import tpu as pltpu
from jax.sharding import PartitionSpec as P

LANES = 128
TILE = 256
WIDE_TILE = 512
PIECES = 4
DEPTH = 3
MESH = pl.DeviceIdType.MESH
LINE = 4
OWN, SIDE_A, SIDE_B, DIAGONAL = range(4)
UP, DOWN = range(2)
TO_A, TO_B, TO_UP, TO_DOWN = range(4)
NEAREST = ((0, 1, 2, 3), (1, 0, 2, 3), (2, 3, 1, 0), (3, 2, 1, 0))
ENDS, INNER, EVERY = (0, LINE - 1), (1, 2), (0, 1, 2, 3)
SLOTS = (
    (OWN, 0), (OWN, 1), (SIDE_A, 0), (SIDE_B, 0), (OWN, 2), (OWN, 3), (SIDE_A, 1), (SIDE_B, 1),
    (SIDE_A, 2), (SIDE_B, 2), (SIDE_A, 3), (SIDE_B, 3),
    (DIAGONAL, 0), (DIAGONAL, 1), (DIAGONAL, 2), (DIAGONAL, 3),
)


def slot_of(line, rank):
    return SLOTS.index((line, rank))


def twin_of(slot):
    line, rank = SLOTS[slot]
    return slot_of({SIDE_A: SIDE_B, SIDE_B: SIDE_A}.get(line, line), rank)


def packed(tokens, routes, route_scores, placement, w_in, w_out):
    tok_rows, feature_cols = tokens.shape
    route_count = routes.shape[1]
    experts = placement.shape[0]
    hidden_units = w_in.shape[3]
    capacity = min(tok_rows, max(2, 2 * tok_rows * route_count // experts))
    slot_total = experts * capacity
    expert_ids = jnp.arange(experts, dtype=jnp.int32)
    route_table = routes[:, :, None] == expert_ids
    physical = jnp.sum(jnp.where(route_table, placement, 0), axis=-1)
    flat_slots = physical.reshape(-1)
    onehot = (flat_slots[:, None] == expert_ids).astype(jnp.int32)
    earlier = jnp.sum((jnp.cumsum(onehot, axis=0) - onehot) * onehot, axis=1)
    position = (flat_slots * capacity + earlier).reshape(tok_rows, route_count)
    slot_index = jnp.arange(slot_total, dtype=jnp.int32)
    placing = jnp.any(position[None, :, :] == slot_index[:, None, None], axis=-1).astype(
        jnp.bfloat16
    )
    outgoing = jnp.dot(placing, tokens, preferred_element_type=jnp.float32).astype(jnp.bfloat16)
    incoming = lax.all_to_all(outgoing, "expert", split_axis=0, concat_axis=0, tiled=True)
    weights_in = w_in[0].reshape(feature_cols, 2 * hidden_units)
    weights_out = w_out[0]
    partial_value = jnp.dot(incoming, weights_in, preferred_element_type=jnp.float32)
    partial_value = partial_value.reshape(slot_total, 2, hidden_units)
    shares = lax.psum_scatter(partial_value, "replica", scatter_dimension=2, tiled=True)
    active = (jax.nn.silu(shares[:, 0]) * shares[:, 1]).astype(jnp.bfloat16)
    result = jnp.dot(
        lax.all_gather(active, "replica", axis=1, tiled=True),
        weights_out,
        preferred_element_type=jnp.float32,
    )
    expert_out = result.astype(jnp.bfloat16)
    returned = lax.all_to_all(expert_out, "expert", split_axis=0, concat_axis=0, tiled=True)
    route_weight = 2.5 * route_scores / jnp.sum(route_scores, axis=1, keepdims=True)
    picked = returned[position.reshape(-1)].reshape(tok_rows, route_count, feature_cols)
    mixed = jnp.sum(picked.astype(jnp.float32) * route_weight[:, :, None], axis=1)
    return mixed.astype(jnp.bfloat16)


def weight_columns(routes_ref, scores_ref, placement_ref):
    routes = routes_ref[...]
    scores = scores_ref[...]
    experts = placement_ref.shape[0]
    physical = jnp.zeros_like(routes)
    for expert in range(experts):
        physical = jnp.where(routes == expert, placement_ref[expert], physical)
    route_weight = 2.5 * scores / jnp.sum(scores, axis=0, keepdims=True)
    column = lax.broadcasted_iota(jnp.int32, (LANES, routes.shape[1]), 0)
    table = jnp.zeros(column.shape, jnp.float32)
    for k in range(routes.shape[0]):
        chosen = physical[k:k + 1, :] == column % experts
        table = jnp.where(chosen, route_weight[k:k + 1, :], table)
    high = table.astype(jnp.bfloat16).astype(jnp.float32)
    middle = (table - high).astype(jnp.bfloat16).astype(jnp.float32)
    low = table - high - middle
    thirds = jnp.where(column < experts, high, jnp.where(column < 2 * experts, middle, low))
    return jnp.where(column < 3 * experts, thirds, 0.0).T.astype(jnp.bfloat16)


def layer_kernel(
    tokens_ref, routes_ref, scores_ref, placement_ref, w_in_ref, w_out_ref, out_ref,
    xs, wg, wu, stage, pairs, wo, contrib, z_in, a_in, b_in, part, sent, got, act,
    t_sem, w_sem, wo_sem, x_send, x_recv, p_send, p_recv,
    z_send, z_recv, a_send, a_recv, b_send, b_recv,
):
    rows, cols = out_ref.shape
    hidden = wg.shape[1]
    own_tokens = pltpu.make_async_copy(tokens_ref, xs.at[0, :, :cols], t_sem)
    own_tokens.start()
    out_weights = pltpu.make_async_copy(w_out_ref.at[0], wo, wo_sem)

    def stage_copy(ct):
        return pltpu.make_async_copy(
            w_in_ref.at[0].reshape(2 * cols, hidden).at[:, pl.ds(ct * LANES, LANES)],
            stage.at[ct % DEPTH], w_sem.at[ct % DEPTH]
        )

    for ct in range(DEPTH):
        stage_copy(ct).start()
    xs[0, :, cols:] = weight_columns(routes_ref, scores_ref, placement_ref)
    tiles = hidden // TILE
    me = lax.axis_index("expert")
    core = lax.axis_index("replica")
    x, y, z = me % 2, (me // 2) % 2, me // 4
    flip_x, flip_y = me + 1 - 2 * x, me + 2 - 4 * y
    near_a = (1 - core) * flip_x + core * flip_y
    near_b = (1 - core) * flip_y + core * flip_x
    chips = (near_a, near_b, me + 4, me - 4)
    sends = {plane: [] for plane in EVERY}

    def on(planes, act_on):
        for plane in planes:
            pl.when(z == plane)(functools.partial(act_on, plane))

    def remote(src, dst, send, recv, chip, on_core=None):
        return pltpu.make_async_remote_copy(
            src_ref=src, dst_ref=dst, send_sem=send, recv_sem=recv,
            device_id=(chip, core if on_core is None else on_core), device_id_type=MESH,
        )

    def arrived(ref, recv):
        remote(ref, ref, a_send.at[0, 0], recv, near_a).wait_recv()

    barrier = pltpu.get_barrier_semaphore()
    for peer in ((near_a, core), (near_b, core), (me, 1 - core)):
        pl.semaphore_signal(barrier, inc=1, device_id=peer, device_id_type=MESH)

    def greet(plane):
        for step, there in ((4, plane + 1), (-4, plane - 1)):
            if 0 <= there < LINE:
                pl.semaphore_signal(
                    barrier, inc=1, device_id=(me + step, core), device_id_type=MESH
                )
        pl.semaphore_wait(barrier, 4 if plane in ENDS else 5)

    on(EVERY, greet)

    def start(plane, copy):
        copy().start()
        sends[plane].append(copy)

    part_rows = rows // 2

    def piece(h):
        return pl.ds(h * part_rows, part_rows)

    def ship(plane, source, from_slot, to_slot, kind, h):
        start(plane, lambda: remote(
            source(), xs.at[to_slot, piece(h)], x_send.at[kind, from_slot, h],
            x_recv.at[to_slot, h], chips[kind]))

    def landed(slot, h):
        arrived(xs.at[slot, piece(h)], x_recv.at[slot, h])
        return lambda: xs.at[slot, piece(h)]

    def ship_along(plane, source, line, rank, h):
        there = NEAREST[plane][rank]
        slot = slot_of(line, rank)
        if plane < LINE - 1 and there <= plane:
            ship(plane, source, slot, slot_of(line, NEAREST[plane + 1].index(there)), TO_UP, h)
        if plane > 0 and there >= plane:
            ship(plane, source, slot, slot_of(line, NEAREST[plane - 1].index(there)), TO_DOWN, h)

    def own_piece(h):
        return xs.at[0, piece(h)]

    def send_own(plane):
        for h in range(2):
            source = functools.partial(own_piece, h)
            ship(plane, source, 0, slot_of(SIDE_A, 0), TO_A, h)
            ship(plane, source, 0, slot_of(SIDE_B, 0), TO_B, h)
            ship_along(plane, source, OWN, 0, h)

    def relay_own(rank, h):
        def act_on(plane):
            slot = slot_of(OWN, rank)
            source = landed(slot, h)
            ship_along(plane, source, OWN, rank, h)
            ship(plane, source, slot, slot_of(SIDE_A, rank), TO_A, h)
            ship(plane, source, slot, slot_of(SIDE_B, rank), TO_B, h)
        return act_on

    def pass_z(rank, h):
        def act_on(plane):
            ship_along(plane, landed(slot_of(OWN, rank), h), OWN, rank, h)
        return act_on

    def pass_ab(rank, h):
        def act_on(plane):
            slot = slot_of(OWN, rank)

            def held():
                return xs.at[slot, piece(h)]

            ship(plane, held, slot, slot_of(SIDE_A, rank), TO_A, h)
            ship(plane, held, slot, slot_of(SIDE_B, rank), TO_B, h)
        return act_on

    def relay_side(h):
        def act_on(plane):
            slot = slot_of(SIDE_A, 0)
            ship(plane, landed(slot, h), slot, slot_of(DIAGONAL, 0), TO_B, h)
        return act_on

    def relay_diagonal(rank, h):
        def act_on(plane):
            ship_along(plane, landed(slot_of(DIAGONAL, rank), h), DIAGONAL, rank, h)
        return act_on

    def land(line, rank, h):
        def act_on(plane):
            landed(slot_of(line, rank), h)
        return act_on

    def sort_tile(ct):
        stage_copy(ct).wait()
        at_cols = slice(ct * LANES, (ct + 1) * LANES)

        flat = stage.at[ct % DEPTH]

        def body(k, carry):
            for n in range(2):
                first = pl.multiple_of((2 * k + n) * LANES, LANES)
                at = pl.ds(first, LANES)
                pairs[n] = flat[pl.ds(2 * first, 2 * LANES), :].astype(jnp.float32)
                wg[at, at_cols] = pairs[n, pl.ds(0, LANES, stride=2), :].astype(jnp.bfloat16)
                wu[at, at_cols] = pairs[n, pl.ds(1, LANES, stride=2), :].astype(jnp.bfloat16)
            return carry

        lax.fori_loop(0, cols // (2 * LANES), body, 0)
        if ct + DEPTH < hidden // LANES:
            stage_copy(ct + DEPTH).start()
        if ct + DEPTH == hidden // LANES:
            out_weights.start()

    def exchange(s, first_slot, count, j):
        at = pl.ds(first_slot * rows, count * rows)
        return remote(sent.at[j, :, at], got.at[j, :, at], p_send.at[s, j], p_recv.at[s, j],
                      me, 1 - core)

    def project_in(s, first_slot, count, j):
        size = count * rows
        at = pl.ds(j * TILE if isinstance(j, int) else pl.multiple_of(j * TILE, TILE), TILE)
        value = xs[pl.ds(first_slot, count), :, :cols].reshape(size, cols)
        for k, weights in ((0, wg), (1, wu)):
            total = jnp.dot(value, weights[:, at], preferred_element_type=jnp.float32)
            part[j, k, :size] = total
            total = total.astype(jnp.bfloat16)
            for n in range(count):
                theirs = pl.ds(twin_of(first_slot + n) * rows, rows)
                sent[j, k, theirs] = total[n * rows:(n + 1) * rows]
        exchange(s, first_slot, count, j).start()

    def activate(first_slot, count, j):
        size = count * rows
        at_rows = pl.ds(first_slot * rows, size)
        gate = part[j, 0, :size] + got[j, 0, at_rows].astype(jnp.float32)
        up = part[j, 1, :size] + got[j, 1, at_rows].astype(jnp.float32)
        at = pl.ds(j * TILE if isinstance(j, int) else pl.multiple_of(j * TILE, TILE), TILE)
        act[:size, at] = (gate / (1.0 + jnp.exp(-gate)) * up).astype(jnp.bfloat16)

    wide_tiles = cols // WIDE_TILE
    per_piece = -(-wide_tiles // PIECES)
    bounds = [min(n * per_piece, wide_tiles) for n in range(PIECES + 1)]
    every_piece = [h for h in range(PIECES) if bounds[h] < bounds[h + 1]]

    def cut(h):
        return pl.ds(bounds[h] * WIDE_TILE, (bounds[h + 1] - bounds[h]) * WIDE_TILE)

    def project_out(first_slot, count, h):
        size = count * rows
        block = pl.ds(first_slot, count)
        lane = lax.broadcasted_iota(jnp.int32, (size, LANES), 1)
        mine = (lane % 16 == me) & (lane < 48)
        scales = xs[block, :, cols:].reshape(size, LANES).astype(jnp.float32)
        scale = jnp.sum(jnp.where(mine, scales, 0.0), axis=1, keepdims=True)

        def body(j, carry):
            at = pl.ds(pl.multiple_of(j * WIDE_TILE, WIDE_TILE), WIDE_TILE)
            value = jnp.dot(act[:size], wo[:, at], preferred_element_type=jnp.float32)
            value = value * scale
            contrib[block, :, at] = value.astype(jnp.bfloat16).reshape(count, rows, WIDE_TILE)
            return carry

        lax.fori_loop(bounds[h], bounds[h + 1], body, 0)

    def add_up(h, target, terms):
        def body(j, carry):
            at = pl.ds(pl.multiple_of(j * WIDE_TILE, WIDE_TILE), WIDE_TILE)
            total = terms[0][:, at].astype(jnp.float32)
            for term in terms[1:]:
                total = total + term[:, at].astype(jnp.float32)
            target[:, at] = total.astype(jnp.bfloat16)
            return carry

        lax.fori_loop(bounds[h], bounds[h + 1], body, 0)

    def pass_sum(plane, h, slot, target, send, recv, chip):
        start(plane, lambda: remote(
            contrib.at[slot, :, cut(h)], target[0].at[target[1]].at[:, cut(h)],
            send.at[(*target[1], h)], recv.at[(*target[1], h)], chip))

    def cross_on(rank, h):
        def act_on(plane):
            pass_sum(plane, h, slot_of(SIDE_B, rank), (a_in, (rank,)), a_send, a_recv, near_a)
            pass_sum(plane, h, slot_of(SIDE_A, rank), (b_in, (rank,)), b_send, b_recv, near_b)
        return act_on

    def straight_on(h):
        def act_on(plane):
            pass_sum(plane, h, slot_of(SIDE_B, 0), (b_in, (0,)), b_send, b_recv, near_b)
        return act_on

    def cross(rank, h):
        cross_on(rank, h)("all")

    def straight(h):
        straight_on(h)("all")

    sends["all"] = []

    def take(buffer, recv, index, h):
        arrived(buffer.at[(*index, slice(None), cut(h))], recv.at[(*index, h)])
        return buffer.at[index]

    def along(line, rank, h):
        kind = line // DIAGONAL

        def act_on(plane):
            there = NEAREST[plane][rank]
            way = UP if there > plane else DOWN
            far = abs(there - plane)
            slot = slot_of(line, rank)
            terms = [contrib.at[slot]]
            if line == DIAGONAL:
                terms.append(take(a_in, a_recv, (rank,), h))
                terms.append(take(b_in, b_recv, (rank,), h))
            if plane != (0 if way == UP else LINE - 1):
                terms.append(take(z_in, z_recv, (kind, way, far), h))
            if len(terms) > 1:
                add_up(h, contrib.at[slot], terms)
            pass_sum(plane, h, slot, (z_in, (kind, way, far - 1)), z_send, z_recv,
                     chips[TO_UP if way == UP else TO_DOWN])
        return act_on

    def from_line(plane, kind, h):
        return [
            take(z_in, z_recv, (kind, way, 0), h)
            for way, stop in ((UP, 0), (DOWN, LINE - 1)) if plane != stop
        ]

    def turn_b(h):
        def act_on(plane):
            slot = slot_of(DIAGONAL, 0)
            add_up(h, contrib.at[slot], [contrib.at[slot], *from_line(plane, 1, h)])
            pass_sum(plane, h, slot, (b_in, (LINE,)), b_send, b_recv, near_b)
        return act_on

    def turn_a_on(h):
        def act_on(plane):
            slot = slot_of(SIDE_A, 0)
            add_up(h, contrib.at[slot], [contrib.at[slot], take(b_in, b_recv, (LINE,), h)])
            pass_sum(plane, h, slot, (a_in, (0,)), a_send, a_recv, near_a)
        return act_on

    def turn_a(h):
        turn_a_on(h)("all")

    def finish(h):
        def act_on(plane):
            terms = [contrib.at[0], take(b_in, b_recv, (0,), h), *from_line(plane, 0, h)]
            add_up(h, out_ref, [*terms, take(a_in, a_recv, (0,), h)])
        return act_on

    def feed(s):
        def body(j, carry):
            project_in(s, *groups[s], j)
            return carry

        lax.fori_loop(0, tiles, body, 0)

    def blend(s):
        def body(j, carry):
            exchange(s, *groups[s], j).wait_recv()
            activate(*groups[s], j)
            return carry

        lax.fori_loop(0, tiles, body, 0)

    def close(s, h):
        project_out(*groups[s], h)

    own_tokens.wait()
    on(EVERY, send_own)
    tiles_in = hidden // LANES
    groups = ((0, 2), (2, 2), (4, 4), (8, 2), (10, 2), (12, 2), (14, 2))
    sort_tile(0)
    sort_tile(1)
    sort_tile(2)
    sort_tile(3)
    on(INNER, pass_z(1, 0))
    on(ENDS, pass_z(1, 0))
    sort_tile(4)
    sort_tile(5)
    on(ENDS, land(SIDE_B, 0, 0))
    on(INNER, relay_side(0))
    on(INNER, pass_z(2, 0))
    on(ENDS, pass_ab(1, 0))
    on(INNER, pass_z(1, 1))
    on(ENDS, relay_side(1))
    on(INNER, pass_ab(1, 0))
    on(ENDS, relay_side(0))
    on(INNER, pass_z(2, 1))
    sort_tile(6)
    on(ENDS, pass_z(1, 1))
    on(INNER, relay_side(1))
    on(ENDS, pass_ab(1, 1))
    on(INNER, land(SIDE_B, 0, 0))
    on(INNER, pass_z(3, 0))
    sort_tile(7)
    on(INNER, pass_ab(1, 1))
    feed(0)
    blend(0)
    out_weights.wait()
    close(0, 2)
    on(ENDS, land(SIDE_B, 0, 1))
    on(INNER, pass_ab(2, 1))
    on(ENDS, along(OWN, 1, 2))
    close(0, 1)
    on(ENDS, land(SIDE_B, 1, 0))
    on(INNER, pass_ab(2, 0))
    close(0, 0)
    on(INNER, pass_z(3, 1))
    on(ENDS, relay_diagonal(0, 0))
    on(ENDS, land(SIDE_A, 1, 1))
    on(INNER, pass_ab(3, 1))
    close(0, 3)
    on(ENDS, pass_z(2, 0))
    on(ENDS, land(SIDE_A, 1, 0))
    on(INNER, land(SIDE_B, 0, 1))
    on(ENDS, along(OWN, 1, 1))
    on(INNER, pass_ab(3, 0))
    on(ENDS, pass_ab(2, 0))
    on(INNER, relay_diagonal(0, 0))
    feed(1)
    on(ENDS, along(OWN, 1, 0))
    on(ENDS, relay_diagonal(0, 1))
    on(INNER, land(SIDE_B, 1, 0))
    on(INNER, land(SIDE_B, 1, 1))
    blend(1)
    on(ENDS, land(SIDE_B, 1, 1))
    close(1, 2)
    on(ENDS, pass_z(2, 1))
    on(ENDS, pass_ab(2, 1))
    close(1, 3)
    on(INNER, relay_diagonal(2, 0))
    on(INNER, land(SIDE_A, 1, 1))
    close(1, 0)
    close(1, 1)
    on(INNER, relay_diagonal(1, 0))
    on(INNER, relay_diagonal(0, 1))
    on(ENDS, pass_z(3, 1))
    on(ENDS, pass_ab(3, 1))
    on(INNER, land(SIDE_A, 1, 0))
    on(ENDS, pass_z(3, 0))
    feed(2)
    on(ENDS, pass_ab(3, 0))
    blend(2)
    on(INNER, straight_on(1))
    close(2, 2)
    on(ENDS, land(SIDE_A, 2, 0))
    on(INNER, land(SIDE_A, 2, 1))
    on(INNER, land(SIDE_B, 2, 0))
    on(ENDS, land(SIDE_B, 2, 1))
    on(INNER, land(SIDE_A, 3, 1))
    close(2, 3)
    on(ENDS, along(OWN, 2, 3))
    close(2, 1)
    on(ENDS, land(SIDE_B, 2, 0))
    on(INNER, land(SIDE_B, 2, 1))
    on(INNER, relay_diagonal(2, 1))
    close(2, 0)
    on(INNER, straight_on(2))
    on(INNER, land(SIDE_A, 2, 0))
    on(ENDS, land(SIDE_A, 2, 1))
    on(ENDS, straight_on(1))
    on(ENDS, along(OWN, 3, 1))
    on(INNER, relay_diagonal(1, 1))
    on(ENDS, along(OWN, 1, 3))
    feed(3)
    on(ENDS, along(OWN, 2, 0))
    on(INNER, straight_on(3))
    on(ENDS, land(SIDE_A, 3, 1))
    on(INNER, along(OWN, 2, 3))
    blend(3)
    on(ENDS, cross_on(1, 2))
    on(ENDS, land(SIDE_A, 3, 0))
    close(3, 1)
    on(ENDS, land(DIAGONAL, 1, 1))
    on(INNER, land(SIDE_B, 3, 1))
    on(INNER, along(OWN, 3, 1))
    close(3, 0)
    on(ENDS, along(OWN, 3, 2))
    on(INNER, cross_on(2, 1))
    close(3, 2)
    on(ENDS, land(DIAGONAL, 1, 0))
    on(INNER, cross_on(1, 1))
    on(ENDS, along(OWN, 2, 2))
    on(INNER, land(SIDE_B, 3, 0))
    on(INNER, relay_diagonal(3, 1))
    on(INNER, land(SIDE_A, 3, 0))
    on(ENDS, along(OWN, 3, 3))
    on(ENDS, cross_on(2, 0))
    on(ENDS, straight_on(2))
    on(INNER, cross_on(1, 0))
    on(ENDS, land(SIDE_B, 3, 0))
    on(INNER, cross_on(2, 2))
    on(ENDS, along(OWN, 2, 1))
    on(ENDS, cross_on(1, 0))
    on(ENDS, land(SIDE_B, 3, 1))
    feed(4)
    on(ENDS, land(DIAGONAL, 2, 0))
    close(3, 3)
    blend(4)
    on(ENDS, along(OWN, 3, 0))
    on(INNER, relay_diagonal(3, 0))
    on(INNER, along(OWN, 2, 0))
    close(4, 0)
    on(INNER, cross_on(2, 0))
    on(INNER, cross_on(3, 0))
    on(INNER, along(OWN, 3, 2))
    close(4, 1)
    on(ENDS, cross_on(3, 0))
    on(ENDS, cross_on(2, 1))
    on(INNER, straight_on(0))
    on(INNER, cross_on(3, 1))
    feed(5)
    on(ENDS, cross_on(3, 1))
    close(4, 2)
    close(4, 3)
    on(INNER, along(OWN, 3, 3))
    on(INNER, along(OWN, 1, 1))
    blend(5)
    on(ENDS, cross_on(3, 3))
    close(5, 3)
    close(5, 2)
    close(5, 1)
    on(INNER, along(OWN, 3, 0))
    on(INNER, cross_on(3, 3))
    on(ENDS, cross_on(1, 1))
    on(INNER, along(OWN, 2, 2))
    on(ENDS, along(DIAGONAL, 1, 2))
    close(5, 0)
    on(ENDS, cross_on(2, 2))
    on(ENDS, cross_on(3, 2))
    on(ENDS, land(DIAGONAL, 3, 1))
    on(ENDS, along(DIAGONAL, 1, 0))
    on(ENDS, land(DIAGONAL, 2, 1))
    on(ENDS, land(DIAGONAL, 3, 0))
    on(INNER, cross_on(2, 3))
    feed(6)
    on(ENDS, straight_on(0))
    blend(6)
    on(INNER, cross_on(3, 2))
    close(6, 0)
    on(ENDS, along(DIAGONAL, 3, 0))
    on(INNER, along(DIAGONAL, 3, 0))
    on(INNER, cross_on(1, 3))
    on(INNER, along(OWN, 1, 0))
    on(ENDS, along(DIAGONAL, 2, 0))
    close(6, 3)
    on(ENDS, along(DIAGONAL, 3, 3))
    on(INNER, along(DIAGONAL, 2, 0))
    on(INNER, along(DIAGONAL, 3, 3))
    on(ENDS, straight_on(3))
    on(INNER, along(DIAGONAL, 1, 0))
    close(6, 1)
    on(ENDS, along(DIAGONAL, 3, 1))
    on(INNER, along(DIAGONAL, 3, 1))
    on(INNER, along(DIAGONAL, 1, 3))
    close(6, 2)
    on(INNER, along(DIAGONAL, 3, 2))
    on(ENDS, along(DIAGONAL, 3, 2))
    on(INNER, cross_on(1, 2))
    on(INNER, along(DIAGONAL, 1, 1))
    on(INNER, turn_b(0))
    on(INNER, along(DIAGONAL, 2, 2))
    on(ENDS, along(DIAGONAL, 2, 2))
    on(INNER, along(DIAGONAL, 1, 2))
    on(ENDS, turn_b(0))
    on(INNER, along(DIAGONAL, 2, 1))
    on(INNER, along(DIAGONAL, 2, 3))
    on(INNER, turn_a_on(0))
    on(INNER, along(OWN, 2, 1))
    on(ENDS, along(DIAGONAL, 2, 1))
    on(ENDS, cross_on(2, 3))
    on(ENDS, along(DIAGONAL, 2, 3))
    on(INNER, turn_b(2))
    on(INNER, along(OWN, 1, 2))
    on(ENDS, along(DIAGONAL, 1, 1))
    on(INNER, along(OWN, 1, 3))
    on(ENDS, cross_on(1, 3))
    on(INNER, turn_b(1))
    on(ENDS, turn_a_on(0))
    on(INNER, turn_a_on(2))
    on(INNER, finish(0))
    on(ENDS, turn_b(3))
    on(INNER, turn_b(3))
    on(ENDS, along(DIAGONAL, 1, 3))
    on(ENDS, turn_b(1))
    on(INNER, turn_a_on(1))
    on(ENDS, turn_a_on(3))
    on(INNER, turn_a_on(3))
    on(ENDS, turn_b(2))
    on(ENDS, turn_a_on(1))
    on(ENDS, turn_a_on(2))
    on(ENDS, finish(0))
    on(INNER, finish(1))
    on(INNER, finish(2))
    on(ENDS, finish(1))
    on(INNER, finish(3))
    on(ENDS, finish(3))
    on(ENDS, finish(2))
    for copy in sends["all"]:
        copy().wait_send()

    def drained(plane):
        for copy in sends[plane]:
            copy().wait_send()

    on(EVERY, drained)
    for s, (first_slot, count) in enumerate(groups):
        def drain(j, carry):
            exchange(s, first_slot, count, j).wait_send()
            return carry

        lax.fori_loop(0, tiles, drain, 0)


def fused(tokens, routes, route_scores, placement, w_in, w_out):
    rows, cols = tokens.shape
    hidden = w_in.shape[3]
    tiles = hidden // TILE
    slots = LINE * LINE
    bf16 = jnp.bfloat16
    dma = pltpu.SemaphoreType.DMA
    return pl.pallas_call(
        layer_kernel,
        out_shape=jax.ShapeDtypeStruct((rows, cols), bf16),
        in_specs=[
            pl.BlockSpec(memory_space=pl.ANY),
            pl.BlockSpec(memory_space=pltpu.VMEM),
            pl.BlockSpec(memory_space=pltpu.VMEM),
            pl.BlockSpec(memory_space=pltpu.SMEM),
            pl.BlockSpec(memory_space=pl.ANY),
            pl.BlockSpec(memory_space=pl.ANY),
        ],
        out_specs=pl.BlockSpec(memory_space=pltpu.VMEM),
        scratch_shapes=[
            pltpu.VMEM((slots, rows, cols + LANES), bf16),
            pltpu.VMEM((cols, hidden), bf16),
            pltpu.VMEM((cols, hidden), bf16),
            pltpu.VMEM((DEPTH, 2 * cols, LANES), bf16),
            pltpu.VMEM((2, 2 * LANES, LANES), jnp.float32),
            pltpu.VMEM((hidden, cols), bf16),
            pltpu.VMEM((slots, rows, cols), bf16),
            pltpu.VMEM((2, 2, LINE - 1, rows, cols), bf16),
            pltpu.VMEM((LINE, rows, cols), bf16),
            pltpu.VMEM((LINE + 1, rows, cols), bf16),
            pltpu.VMEM((tiles, 2, LINE * rows, TILE), jnp.float32),
            pltpu.VMEM((tiles, 2, slots * rows, TILE), bf16),
            pltpu.VMEM((tiles, 2, slots * rows, TILE), bf16),
            pltpu.VMEM((LINE * rows, hidden), bf16),
            dma, dma((DEPTH,)), dma, dma((4, slots, 2)), dma((slots, 2)),
            dma((slots, tiles)), dma((slots, tiles)),
            dma((2, 2, LINE - 1, PIECES)), dma((2, 2, LINE - 1, PIECES)),
            dma((LINE, PIECES)), dma((LINE, PIECES)),
            dma((LINE + 1, PIECES)), dma((LINE + 1, PIECES)),
        ],
        compiler_params=pltpu.CompilerParams(
            collective_id=0, has_side_effects=True, vmem_limit_bytes=67043328
        ),
    )(tokens, routes.T, route_scores.T, placement, w_in, w_out)


def on_device(tokens, routes, route_scores, placement, w_in, w_out):
    tok_rows = tokens.shape[0]
    experts = placement.shape[0]
    fits = experts == 4 * LINE and lax.axis_size("replica") == 2
    if fits and 2 * tok_rows * routes.shape[1] // experts >= tok_rows:
        return fused(tokens, routes, route_scores, placement, w_in, w_out)
    return packed(tokens, routes, route_scores, placement, w_in, w_out)


def solution(mesh):
    in_specs = (
        P("expert", "replica"),
        P("expert", None),
        P("expert", None),
        P(),
        P("expert", "replica", None, None),
        P("expert", None, "replica"),
    )
    out_specs = P("expert", "replica")
    return jax.shard_map(
        on_device, mesh=mesh, in_specs=in_specs, out_specs=out_specs, check_vma=False
    )
```

```python
import functools

import jax
import jax.numpy as jnp
from jax import lax
from jax.experimental import pallas as pl
from jax.experimental.pallas import tpu as pltpu
from jax.sharding import PartitionSpec as P

LANES = 128
TILE = 256
WIDE_TILE = 512
PIECES = 4
DEPTH = 3
MESH = pl.DeviceIdType.MESH
LINE = 4
OWN, SIDE_A, SIDE_B, DIAGONAL = range(4)
UP, DOWN = range(2)
TO_A, TO_B, TO_UP, TO_DOWN = range(4)
NEAREST = ((0, 1, 2, 3), (1, 0, 2, 3), (2, 3, 1, 0), (3, 2, 1, 0))
ENDS, INNER, EVERY = (0, LINE - 1), (1, 2), (0, 1, 2, 3)
SLOTS = (
    (OWN, 0), (OWN, 1), (SIDE_A, 0), (SIDE_B, 0), (OWN, 2), (OWN, 3), (SIDE_A, 1), (SIDE_B, 1),
    (SIDE_A, 2), (SIDE_B, 2), (SIDE_A, 3), (SIDE_B, 3),
    (DIAGONAL, 0), (DIAGONAL, 1), (DIAGONAL, 2), (DIAGONAL, 3),
)


def slot_of(line, rank):
    return SLOTS.index((line, rank))


def twin_of(slot):
    line, rank = SLOTS[slot]
    return slot_of({SIDE_A: SIDE_B, SIDE_B: SIDE_A}.get(line, line), rank)


def packed(tokens, routes, route_scores, placement, w_in, w_out):
    tok_rows, feature_cols = tokens.shape
    route_count = routes.shape[1]
    experts = placement.shape[0]
    hidden_units = w_in.shape[3]
    capacity = min(tok_rows, max(2, 2 * tok_rows * route_count // experts))
    slot_total = experts * capacity
    expert_ids = jnp.arange(experts, dtype=jnp.int32)
    route_table = routes[:, :, None] == expert_ids
    physical = jnp.sum(jnp.where(route_table, placement, 0), axis=-1)
    flat_slots = physical.reshape(-1)
    onehot = (flat_slots[:, None] == expert_ids).astype(jnp.int32)
    earlier = jnp.sum((jnp.cumsum(onehot, axis=0) - onehot) * onehot, axis=1)
    position = (flat_slots * capacity + earlier).reshape(tok_rows, route_count)
    slot_index = jnp.arange(slot_total, dtype=jnp.int32)
    placing = jnp.any(position[None, :, :] == slot_index[:, None, None], axis=-1).astype(
        jnp.bfloat16
    )
    outgoing = jnp.dot(placing, tokens, preferred_element_type=jnp.float32).astype(jnp.bfloat16)
    incoming = lax.all_to_all(outgoing, "expert", split_axis=0, concat_axis=0, tiled=True)
    weights_in = w_in[0].reshape(feature_cols, 2 * hidden_units)
    weights_out = w_out[0]
    partial_value = jnp.dot(incoming, weights_in, preferred_element_type=jnp.float32)
    partial_value = partial_value.reshape(slot_total, 2, hidden_units)
    shares = lax.psum_scatter(partial_value, "replica", scatter_dimension=2, tiled=True)
    active = (jax.nn.silu(shares[:, 0]) * shares[:, 1]).astype(jnp.bfloat16)
    result = jnp.dot(
        lax.all_gather(active, "replica", axis=1, tiled=True),
        weights_out,
        preferred_element_type=jnp.float32,
    )
    expert_out = result.astype(jnp.bfloat16)
    returned = lax.all_to_all(expert_out, "expert", split_axis=0, concat_axis=0, tiled=True)
    route_weight = 2.5 * route_scores / jnp.sum(route_scores, axis=1, keepdims=True)
    picked = returned[position.reshape(-1)].reshape(tok_rows, route_count, feature_cols)
    mixed = jnp.sum(picked.astype(jnp.float32) * route_weight[:, :, None], axis=1)
    return mixed.astype(jnp.bfloat16)


def weight_columns(routes_ref, scores_ref, placement_ref):
    routes = routes_ref[...]
    scores = scores_ref[...]
    experts = placement_ref.shape[0]
    physical = jnp.zeros_like(routes)
    for expert in range(experts):
        physical = jnp.where(routes == expert, placement_ref[expert], physical)
    route_weight = 2.5 * scores / jnp.sum(scores, axis=0, keepdims=True)
    column = lax.broadcasted_iota(jnp.int32, (LANES, routes.shape[1]), 0)
    table = jnp.zeros(column.shape, jnp.float32)
    for k in range(routes.shape[0]):
        chosen = physical[k:k + 1, :] == column % experts
        table = jnp.where(chosen, route_weight[k:k + 1, :], table)
    high = table.astype(jnp.bfloat16).astype(jnp.float32)
    middle = (table - high).astype(jnp.bfloat16).astype(jnp.float32)
    low = table - high - middle
    thirds = jnp.where(column < experts, high, jnp.where(column < 2 * experts, middle, low))
    return jnp.where(column < 3 * experts, thirds, 0.0).T.astype(jnp.bfloat16)


def layer_kernel(
    tokens_ref, routes_ref, scores_ref, placement_ref, w_in_ref, w_out_ref, out_ref,
    xs, wg, wu, stage, pairs, wo, contrib, z_in, a_in, b_in, part, sent, got, act,
    t_sem, w_sem, wo_sem, x_send, x_recv, p_send, p_recv,
    z_send, z_recv, a_send, a_recv, b_send, b_recv,
):
    rows, cols = out_ref.shape
    hidden = wg.shape[1]
    own_tokens = pltpu.make_async_copy(tokens_ref, xs.at[0, :, :cols], t_sem)
    own_tokens.start()
    out_weights = pltpu.make_async_copy(w_out_ref.at[0], wo, wo_sem)

    def stage_copy(ct):
        return pltpu.make_async_copy(
            w_in_ref.at[0].reshape(2 * cols, hidden).at[:, pl.ds(ct * LANES, LANES)],
            stage.at[ct % DEPTH], w_sem.at[ct % DEPTH]
        )

    for ct in range(DEPTH):
        stage_copy(ct).start()
    xs[0, :, cols:] = weight_columns(routes_ref, scores_ref, placement_ref)
    tiles = hidden // TILE
    me = lax.axis_index("expert")
    core = lax.axis_index("replica")
    x, y, z = me % 2, (me // 2) % 2, me // 4
    flip_x, flip_y = me + 1 - 2 * x, me + 2 - 4 * y
    near_a = (1 - core) * flip_x + core * flip_y
    near_b = (1 - core) * flip_y + core * flip_x
    chips = (near_a, near_b, me + 4, me - 4)
    sends = {plane: [] for plane in EVERY}

    def on(planes, act_on):
        for plane in planes:
            pl.when(z == plane)(functools.partial(act_on, plane))

    def remote(src, dst, send, recv, chip, on_core=None):
        return pltpu.make_async_remote_copy(
            src_ref=src, dst_ref=dst, send_sem=send, recv_sem=recv,
            device_id=(chip, core if on_core is None else on_core), device_id_type=MESH,
        )

    def arrived(ref, recv):
        remote(ref, ref, a_send.at[0, 0], recv, near_a).wait_recv()

    barrier = pltpu.get_barrier_semaphore()
    for peer in ((near_a, core), (near_b, core), (me, 1 - core)):
        pl.semaphore_signal(barrier, inc=1, device_id=peer, device_id_type=MESH)

    def greet(plane):
        for step, there in ((4, plane + 1), (-4, plane - 1)):
            if 0 <= there < LINE:
                pl.semaphore_signal(
                    barrier, inc=1, device_id=(me + step, core), device_id_type=MESH
                )
        pl.semaphore_wait(barrier, 4 if plane in ENDS else 5)

    on(EVERY, greet)

    def start(plane, copy):
        copy().start()
        sends[plane].append(copy)

    part_rows = rows // 2

    def piece(h):
        return pl.ds(h * part_rows, part_rows)

    def ship(plane, source, from_slot, to_slot, kind, h):
        start(plane, lambda: remote(
            source(), xs.at[to_slot, piece(h)], x_send.at[kind, from_slot, h],
            x_recv.at[to_slot, h], chips[kind]))

    def landed(slot, h):
        arrived(xs.at[slot, piece(h)], x_recv.at[slot, h])
        return lambda: xs.at[slot, piece(h)]

    def ship_along(plane, source, line, rank, h):
        there = NEAREST[plane][rank]
        slot = slot_of(line, rank)
        if plane < LINE - 1 and there <= plane:
            ship(plane, source, slot, slot_of(line, NEAREST[plane + 1].index(there)), TO_UP, h)
        if plane > 0 and there >= plane:
            ship(plane, source, slot, slot_of(line, NEAREST[plane - 1].index(there)), TO_DOWN, h)

    def own_piece(h):
        return xs.at[0, piece(h)]

    def send_own(plane):
        for h in range(2):
            source = functools.partial(own_piece, h)
            ship(plane, source, 0, slot_of(SIDE_A, 0), TO_A, h)
            ship(plane, source, 0, slot_of(SIDE_B, 0), TO_B, h)
            ship_along(plane, source, OWN, 0, h)

    def relay_own(rank, h):
        def act_on(plane):
            slot = slot_of(OWN, rank)
            source = landed(slot, h)
            ship_along(plane, source, OWN, rank, h)
            ship(plane, source, slot, slot_of(SIDE_A, rank), TO_A, h)
            ship(plane, source, slot, slot_of(SIDE_B, rank), TO_B, h)
        return act_on

    def pass_z(rank, h):
        def act_on(plane):
            ship_along(plane, landed(slot_of(OWN, rank), h), OWN, rank, h)
        return act_on

    def pass_ab(rank, h):
        def act_on(plane):
            slot = slot_of(OWN, rank)

            def held():
                return xs.at[slot, piece(h)]

            ship(plane, held, slot, slot_of(SIDE_A, rank), TO_A, h)
            ship(plane, held, slot, slot_of(SIDE_B, rank), TO_B, h)
        return act_on

    def relay_side(h):
        def act_on(plane):
            slot = slot_of(SIDE_A, 0)
            ship(plane, landed(slot, h), slot, slot_of(DIAGONAL, 0), TO_B, h)
        return act_on

    def relay_diagonal(rank, h):
        def act_on(plane):
            ship_along(plane, landed(slot_of(DIAGONAL, rank), h), DIAGONAL, rank, h)
        return act_on

    def land(line, rank, h):
        def act_on(plane):
            landed(slot_of(line, rank), h)
        return act_on

    def sort_tile(ct):
        stage_copy(ct).wait()
        at_cols = slice(ct * LANES, (ct + 1) * LANES)

        flat = stage.at[ct % DEPTH]

        def body(k, carry):
            for n in range(2):
                first = pl.multiple_of((2 * k + n) * LANES, LANES)
                at = pl.ds(first, LANES)
                pairs[n] = flat[pl.ds(2 * first, 2 * LANES), :].astype(jnp.float32)
                wg[at, at_cols] = pairs[n, pl.ds(0, LANES, stride=2), :].astype(jnp.bfloat16)
                wu[at, at_cols] = pairs[n, pl.ds(1, LANES, stride=2), :].astype(jnp.bfloat16)
            return carry

        lax.fori_loop(0, cols // (2 * LANES), body, 0)
        if ct + DEPTH < hidden // LANES:
            stage_copy(ct + DEPTH).start()
        if ct + DEPTH == hidden // LANES:
            out_weights.start()

    def exchange(s, first_slot, count, j):
        at = pl.ds(first_slot * rows, count * rows)
        return remote(sent.at[j, :, at], got.at[j, :, at], p_send.at[s, j], p_recv.at[s, j],
                      me, 1 - core)

    def project_in(s, first_slot, count, j):
        size = count * rows
        at = pl.ds(j * TILE if isinstance(j, int) else pl.multiple_of(j * TILE, TILE), TILE)
        value = xs[pl.ds(first_slot, count), :, :cols].reshape(size, cols)
        for k, weights in ((0, wg), (1, wu)):
            total = jnp.dot(value, weights[:, at], preferred_element_type=jnp.float32)
            part[j, k, :size] = total
            total = total.astype(jnp.bfloat16)
            for n in range(count):
                theirs = pl.ds(twin_of(first_slot + n) * rows, rows)
                sent[j, k, theirs] = total[n * rows:(n + 1) * rows]
        exchange(s, first_slot, count, j).start()

    def activate(first_slot, count, j):
        size = count * rows
        at_rows = pl.ds(first_slot * rows, size)
        gate = part[j, 0, :size] + got[j, 0, at_rows].astype(jnp.float32)
        up = part[j, 1, :size] + got[j, 1, at_rows].astype(jnp.float32)
        at = pl.ds(j * TILE if isinstance(j, int) else pl.multiple_of(j * TILE, TILE), TILE)
        act[:size, at] = (gate / (1.0 + jnp.exp(-gate)) * up).astype(jnp.bfloat16)

    wide_tiles = cols // WIDE_TILE
    per_piece = -(-wide_tiles // PIECES)
    bounds = [min(n * per_piece, wide_tiles) for n in range(PIECES + 1)]
    every_piece = [h for h in range(PIECES) if bounds[h] < bounds[h + 1]]

    def cut(h):
        return pl.ds(bounds[h] * WIDE_TILE, (bounds[h + 1] - bounds[h]) * WIDE_TILE)

    def project_out(first_slot, count, h):
        size = count * rows
        block = pl.ds(first_slot, count)
        lane = lax.broadcasted_iota(jnp.int32, (size, LANES), 1)
        mine = (lane % 16 == me) & (lane < 48)
        scales = xs[block, :, cols:].reshape(size, LANES).astype(jnp.float32)
        scale = jnp.sum(jnp.where(mine, scales, 0.0), axis=1, keepdims=True)

        def body(j, carry):
            at = pl.ds(pl.multiple_of(j * WIDE_TILE, WIDE_TILE), WIDE_TILE)
            value = jnp.dot(act[:size], wo[:, at], preferred_element_type=jnp.float32)
            value = value * scale
            contrib[block, :, at] = value.astype(jnp.bfloat16).reshape(count, rows, WIDE_TILE)
            return carry

        lax.fori_loop(bounds[h], bounds[h + 1], body, 0)

    def add_up(h, target, terms):
        def body(j, carry):
            at = pl.ds(pl.multiple_of(j * WIDE_TILE, WIDE_TILE), WIDE_TILE)
            total = terms[0][:, at].astype(jnp.float32)
            for term in terms[1:]:
                total = total + term[:, at].astype(jnp.float32)
            target[:, at] = total.astype(jnp.bfloat16)
            return carry

        lax.fori_loop(bounds[h], bounds[h + 1], body, 0)

    def pass_sum(plane, h, slot, target, send, recv, chip):
        start(plane, lambda: remote(
            contrib.at[slot, :, cut(h)], target[0].at[target[1]].at[:, cut(h)],
            send.at[(*target[1], h)], recv.at[(*target[1], h)], chip))

    def cross_on(rank, h):
        def act_on(plane):
            pass_sum(plane, h, slot_of(SIDE_B, rank), (a_in, (rank,)), a_send, a_recv, near_a)
            pass_sum(plane, h, slot_of(SIDE_A, rank), (b_in, (rank,)), b_send, b_recv, near_b)
        return act_on

    def straight_on(h):
        def act_on(plane):
            pass_sum(plane, h, slot_of(SIDE_B, 0), (b_in, (0,)), b_send, b_recv, near_b)
        return act_on

    def cross(rank, h):
        cross_on(rank, h)("all")

    def straight(h):
        straight_on(h)("all")

    sends["all"] = []

    def take(buffer, recv, index, h):
        arrived(buffer.at[(*index, slice(None), cut(h))], recv.at[(*index, h)])
        return buffer.at[index]

    def along(line, rank, h):
        kind = line // DIAGONAL

        def act_on(plane):
            there = NEAREST[plane][rank]
            way = UP if there > plane else DOWN
            far = abs(there - plane)
            slot = slot_of(line, rank)
            terms = [contrib.at[slot]]
            if line == DIAGONAL:
                terms.append(take(a_in, a_recv, (rank,), h))
                terms.append(take(b_in, b_recv, (rank,), h))
            if plane != (0 if way == UP else LINE - 1):
                terms.append(take(z_in, z_recv, (kind, way, far), h))
            if len(terms) > 1:
                add_up(h, contrib.at[slot], terms)
            pass_sum(plane, h, slot, (z_in, (kind, way, far - 1)), z_send, z_recv,
                     chips[TO_UP if way == UP else TO_DOWN])
        return act_on

    def from_line(plane, kind, h):
        return [
            take(z_in, z_recv, (kind, way, 0), h)
            for way, stop in ((UP, 0), (DOWN, LINE - 1)) if plane != stop
        ]

    def turn_b(h):
        def act_on(plane):
            slot = slot_of(DIAGONAL, 0)
            add_up(h, contrib.at[slot], [contrib.at[slot], *from_line(plane, 1, h)])
            pass_sum(plane, h, slot, (b_in, (LINE,)), b_send, b_recv, near_b)
        return act_on

    def turn_a_on(h):
        def act_on(plane):
            slot = slot_of(SIDE_A, 0)
            add_up(h, contrib.at[slot], [contrib.at[slot], take(b_in, b_recv, (LINE,), h)])
            pass_sum(plane, h, slot, (a_in, (0,)), a_send, a_recv, near_a)
        return act_on

    def turn_a(h):
        turn_a_on(h)("all")

    def finish(h):
        def act_on(plane):
            terms = [contrib.at[0], take(b_in, b_recv, (0,), h), *from_line(plane, 0, h)]
            add_up(h, out_ref, [*terms, take(a_in, a_recv, (0,), h)])
        return act_on

    def feed(s):
        def body(j, carry):
            project_in(s, *groups[s], j)
            return carry

        lax.fori_loop(0, tiles, body, 0)

    def blend(s):
        def body(j, carry):
            exchange(s, *groups[s], j).wait_recv()
            activate(*groups[s], j)
            return carry

        lax.fori_loop(0, tiles, body, 0)

    def close(s, h):
        project_out(*groups[s], h)

    own_tokens.wait()
    on(EVERY, send_own)
    tiles_in = hidden // LANES
    groups = ((0, 2), (2, 2), (4, 4), (8, 2), (10, 2), (12, 2), (14, 2))
    sort_tile(0)
    sort_tile(1)
    sort_tile(2)
    sort_tile(3)
    on(INNER, pass_z(1, 0))
    on(ENDS, pass_z(1, 0))
    sort_tile(4)
    sort_tile(5)
    on(INNER, pass_z(2, 0))
    on(ENDS, land(SIDE_B, 0, 0))
    on(INNER, relay_side(0))
    on(ENDS, pass_ab(1, 0))
    on(INNER, pass_z(1, 1))
    on(ENDS, relay_side(1))
    on(INNER, pass_ab(1, 0))
    on(ENDS, relay_side(0))
    on(INNER, relay_side(1))
    on(INNER, pass_z(2, 1))
    sort_tile(6)
    on(ENDS, pass_z(1, 1))
    on(ENDS, pass_ab(1, 1))
    on(INNER, land(SIDE_B, 0, 0))
    on(INNER, pass_z(3, 0))
    sort_tile(7)
    on(INNER, pass_ab(1, 1))
    on(INNER, pass_ab(2, 1))
    feed(0)
    blend(0)
    out_weights.wait()
    close(0, 2)
    on(ENDS, land(SIDE_B, 0, 1))
    on(ENDS, along(OWN, 1, 2))
    close(0, 1)
    on(ENDS, land(SIDE_B, 1, 0))
    on(INNER, pass_ab(2, 0))
    close(0, 0)
    on(INNER, pass_z(3, 1))
    on(ENDS, relay_diagonal(0, 0))
    on(ENDS, land(SIDE_A, 1, 1))
    on(INNER, pass_ab(3, 1))
    close(0, 3)
    on(ENDS, pass_z(2, 0))
    on(ENDS, land(SIDE_A, 1, 0))
    on(INNER, land(SIDE_B, 0, 1))
    on(ENDS, along(OWN, 1, 1))
    on(INNER, pass_ab(3, 0))
    on(ENDS, pass_ab(2, 0))
    on(INNER, relay_diagonal(0, 0))
    feed(1)
    on(ENDS, along(OWN, 1, 0))
    on(ENDS, relay_diagonal(0, 1))
    on(INNER, relay_diagonal(0, 1))
    on(INNER, land(SIDE_B, 1, 0))
    on(INNER, land(SIDE_B, 1, 1))
    blend(1)
    on(ENDS, land(SIDE_B, 1, 1))
    close(1, 2)
    on(ENDS, pass_z(2, 1))
    on(ENDS, pass_ab(2, 1))
    close(1, 3)
    on(INNER, relay_diagonal(2, 0))
    on(INNER, land(SIDE_A, 1, 1))
    close(1, 0)
    close(1, 1)
    on(INNER, relay_diagonal(1, 0))
    on(ENDS, pass_z(3, 1))
    on(ENDS, pass_ab(3, 1))
    on(INNER, land(SIDE_A, 1, 0))
    on(ENDS, pass_z(3, 0))
    feed(2)
    on(ENDS, pass_ab(3, 0))
    blend(2)
    on(INNER, straight_on(1))
    close(2, 2)
    on(ENDS, land(SIDE_A, 2, 0))
    on(INNER, land(SIDE_A, 2, 1))
    on(ENDS, land(SIDE_B, 2, 1))
    close(2, 3)
    on(INNER, land(SIDE_B, 2, 0))
    on(INNER, land(SIDE_A, 3, 1))
    on(ENDS, along(OWN, 2, 3))
    close(2, 1)
    on(INNER, straight_on(2))
    on(ENDS, land(SIDE_B, 2, 0))
    on(INNER, relay_diagonal(2, 1))
    on(INNER, land(SIDE_B, 2, 1))
    close(2, 0)
    on(ENDS, land(SIDE_A, 2, 1))
    on(ENDS, along(OWN, 3, 1))
    on(INNER, relay_diagonal(1, 1))
    on(INNER, land(SIDE_A, 2, 0))
    on(ENDS, along(OWN, 1, 3))
    feed(3)
    on(ENDS, along(OWN, 2, 0))
    on(ENDS, straight_on(1))
    on(INNER, straight_on(3))
    on(ENDS, land(SIDE_A, 3, 1))
    on(INNER, along(OWN, 2, 3))
    blend(3)
    on(ENDS, cross_on(1, 2))
    on(ENDS, land(SIDE_A, 3, 0))
    close(3, 1)
    on(ENDS, land(DIAGONAL, 1, 1))
    on(INNER, along(OWN, 3, 1))
    on(INNER, cross_on(2, 1))
    close(3, 2)
    on(ENDS, land(DIAGONAL, 1, 0))
    on(INNER, cross_on(1, 1))
    close(3, 0)
    on(ENDS, along(OWN, 3, 2))
    on(ENDS, along(OWN, 2, 2))
    on(INNER, land(SIDE_B, 3, 1))
    on(INNER, land(SIDE_A, 3, 0))
    on(ENDS, along(OWN, 3, 3))
    on(ENDS, cross_on(2, 0))
    on(ENDS, land(SIDE_B, 3, 0))
    on(ENDS, along(OWN, 2, 1))
    on(ENDS, cross_on(1, 0))
    on(INNER, land(SIDE_B, 3, 0))
    on(INNER, relay_diagonal(3, 1))
    on(INNER, cross_on(2, 2))
    on(ENDS, land(SIDE_B, 3, 1))
    feed(4)
    on(ENDS, straight_on(2))
    on(INNER, cross_on(1, 0))
    on(ENDS, land(DIAGONAL, 2, 0))
    close(3, 3)
    blend(4)
    on(ENDS, along(OWN, 3, 0))
    on(INNER, relay_diagonal(3, 0))
    on(INNER, along(OWN, 2, 0))
    close(4, 0)
    on(INNER, cross_on(2, 0))
    on(INNER, cross_on(3, 0))
    on(INNER, along(OWN, 3, 2))
    close(4, 1)
    on(ENDS, cross_on(3, 0))
    on(ENDS, cross_on(2, 1))
    feed(5)
    on(ENDS, cross_on(3, 1))
    on(INNER, cross_on(2, 3))
    close(4, 2)
    on(INNER, straight_on(0))
    on(INNER, cross_on(3, 1))
    close(4, 3)
    on(INNER, along(OWN, 3, 3))
    on(INNER, along(OWN, 1, 1))
    on(ENDS, cross_on(3, 3))
    blend(5)
    close(5, 3)
    close(5, 2)
    close(5, 1)
    on(INNER, along(OWN, 3, 0))
    on(ENDS, cross_on(1, 1))
    on(INNER, cross_on(3, 3))
    on(INNER, along(OWN, 2, 2))
    on(ENDS, along(DIAGONAL, 1, 2))
    close(5, 0)
    on(ENDS, cross_on(2, 2))
    on(ENDS, cross_on(3, 2))
    on(ENDS, land(DIAGONAL, 3, 1))
    on(ENDS, along(DIAGONAL, 1, 0))
    on(ENDS, land(DIAGONAL, 2, 1))
    on(ENDS, land(DIAGONAL, 3, 0))
    feed(6)
    on(ENDS, straight_on(0))
    blend(6)
    on(INNER, cross_on(3, 2))
    close(6, 0)
    on(ENDS, along(DIAGONAL, 3, 0))
    on(INNER, along(DIAGONAL, 3, 0))
    on(INNER, cross_on(1, 3))
    on(INNER, along(OWN, 1, 0))
    on(ENDS, along(DIAGONAL, 2, 0))
    close(6, 3)
    on(ENDS, along(DIAGONAL, 3, 3))
    on(INNER, along(DIAGONAL, 2, 0))
    on(INNER, along(DIAGONAL, 3, 3))
    on(ENDS, cross_on(2, 3))
    on(ENDS, straight_on(3))
    on(INNER, along(DIAGONAL, 1, 0))
    close(6, 1)
    on(ENDS, along(DIAGONAL, 3, 1))
    on(INNER, along(DIAGONAL, 3, 1))
    on(INNER, along(DIAGONAL, 1, 3))
    close(6, 2)
    on(INNER, along(DIAGONAL, 3, 2))
    on(ENDS, along(DIAGONAL, 3, 2))
    on(INNER, cross_on(1, 2))
    on(INNER, along(DIAGONAL, 1, 1))
    on(INNER, turn_b(0))
    on(INNER, along(DIAGONAL, 2, 2))
    on(ENDS, along(DIAGONAL, 2, 2))
    on(INNER, along(DIAGONAL, 1, 2))
    on(INNER, along(DIAGONAL, 2, 1))
    on(INNER, along(DIAGONAL, 2, 3))
    on(INNER, turn_a_on(0))
    on(INNER, along(OWN, 2, 1))
    on(ENDS, along(DIAGONAL, 2, 1))
    on(ENDS, turn_b(0))
    on(ENDS, along(DIAGONAL, 2, 3))
    on(INNER, turn_b(2))
    on(INNER, along(OWN, 1, 2))
    on(ENDS, along(DIAGONAL, 1, 1))
    on(INNER, along(OWN, 1, 3))
    on(ENDS, cross_on(1, 3))
    on(INNER, turn_b(1))
    on(ENDS, turn_a_on(0))
    on(INNER, turn_a_on(2))
    on(INNER, finish(0))
    on(ENDS, along(DIAGONAL, 1, 3))
    on(ENDS, turn_b(3))
    on(INNER, turn_b(3))
    on(INNER, turn_a_on(1))
    on(ENDS, turn_b(1))
    on(ENDS, turn_a_on(3))
    on(INNER, turn_a_on(3))
    on(ENDS, turn_b(2))
    on(ENDS, turn_a_on(1))
    on(ENDS, turn_a_on(2))
    on(ENDS, finish(0))
    on(INNER, finish(1))
    on(INNER, finish(2))
    on(ENDS, finish(1))
    on(INNER, finish(3))
    on(ENDS, finish(3))
    on(ENDS, finish(2))
    for copy in sends["all"]:
        copy().wait_send()

    def drained(plane):
        for copy in sends[plane]:
            copy().wait_send()

    on(EVERY, drained)
    for s, (first_slot, count) in enumerate(groups):
        def drain(j, carry):
            exchange(s, first_slot, count, j).wait_send()
            return carry

        lax.fori_loop(0, tiles, drain, 0)


def fused(tokens, routes, route_scores, placement, w_in, w_out):
    rows, cols = tokens.shape
    hidden = w_in.shape[3]
    tiles = hidden // TILE
    slots = LINE * LINE
    bf16 = jnp.bfloat16
    dma = pltpu.SemaphoreType.DMA
    return pl.pallas_call(
        layer_kernel,
        out_shape=jax.ShapeDtypeStruct((rows, cols), bf16),
        in_specs=[
            pl.BlockSpec(memory_space=pl.ANY),
            pl.BlockSpec(memory_space=pltpu.VMEM),
            pl.BlockSpec(memory_space=pltpu.VMEM),
            pl.BlockSpec(memory_space=pltpu.SMEM),
            pl.BlockSpec(memory_space=pl.ANY),
            pl.BlockSpec(memory_space=pl.ANY),
        ],
        out_specs=pl.BlockSpec(memory_space=pltpu.VMEM),
        scratch_shapes=[
            pltpu.VMEM((slots, rows, cols + LANES), bf16),
            pltpu.VMEM((cols, hidden), bf16),
            pltpu.VMEM((cols, hidden), bf16),
            pltpu.VMEM((DEPTH, 2 * cols, LANES), bf16),
            pltpu.VMEM((2, 2 * LANES, LANES), jnp.float32),
            pltpu.VMEM((hidden, cols), bf16),
            pltpu.VMEM((slots, rows, cols), bf16),
            pltpu.VMEM((2, 2, LINE - 1, rows, cols), bf16),
            pltpu.VMEM((LINE, rows, cols), bf16),
            pltpu.VMEM((LINE + 1, rows, cols), bf16),
            pltpu.VMEM((tiles, 2, LINE * rows, TILE), jnp.float32),
            pltpu.VMEM((tiles, 2, slots * rows, TILE), bf16),
            pltpu.VMEM((tiles, 2, slots * rows, TILE), bf16),
            pltpu.VMEM((LINE * rows, hidden), bf16),
            dma, dma((DEPTH,)), dma, dma((4, slots, 2)), dma((slots, 2)),
            dma((slots, tiles)), dma((slots, tiles)),
            dma((2, 2, LINE - 1, PIECES)), dma((2, 2, LINE - 1, PIECES)),
            dma((LINE, PIECES)), dma((LINE, PIECES)),
            dma((LINE + 1, PIECES)), dma((LINE + 1, PIECES)),
        ],
        compiler_params=pltpu.CompilerParams(
            collective_id=0, has_side_effects=True, vmem_limit_bytes=67043328
        ),
    )(tokens, routes.T, route_scores.T, placement, w_in, w_out)


def on_device(tokens, routes, route_scores, placement, w_in, w_out):
    tok_rows = tokens.shape[0]
    experts = placement.shape[0]
    fits = experts == 4 * LINE and lax.axis_size("replica") == 2
    if fits and 2 * tok_rows * routes.shape[1] // experts >= tok_rows:
        return fused(tokens, routes, route_scores, placement, w_in, w_out)
    return packed(tokens, routes, route_scores, placement, w_in, w_out)


def solution(mesh):
    in_specs = (
        P("expert", "replica"),
        P("expert", None),
        P("expert", None),
        P(),
        P("expert", "replica", None, None),
        P("expert", None, "replica"),
    )
    out_specs = P("expert", "replica")
    return jax.shard_map(
        on_device, mesh=mesh, in_specs=in_specs, out_specs=out_specs, check_vma=False
    )
```
